32 devices in a mesh: grp: 2 (over x), blk: 16 (over z, y, core).
Axes of the slice: x: 2, y: 2, z: 4, core: 2. Of those that a mesh axis runs over, the one named last changes fastest.
Arguments:
- sketch: bfloat16 [256, 131072], P(None, 'blk'), may hold values from -3 to 3
- leaf_maps: bfloat16 [2, 16, 256, 256], P('grp', 'blk')
- mix_maps: bfloat16 [2, 64, 16, 16], P('grp', 'blk')
Outputs:
- sketch_update: bfloat16 [256, 131072], P('grp', 'blk')
The draws below stay inside these ranges and needn't reach their ends.
All inputs are finite; a program needn't handle non-finite values.
Results may differ from the reference program's by a relative error of at most 0.015.
Values may be sent and summed in bfloat16 or wider, within the bound.
A program may use at most 64 MiB of HBM per device.

```python
import math
import jax
import jax.numpy as jnp
from jax import lax

B = 128
R = 256
A = 64
N = 131072
N_GRP = 2
N_BLK = 16


def draw_leaf_maps(key, part):
    leaf_side = 2 * B
    full_shape = (N_GRP, N_BLK, leaf_side, leaf_side)
    random_part = jax.random.normal(key, full_shape, jnp.float32)
    identity = jnp.eye(leaf_side, dtype=jnp.float32)
    return (identity + 0.3 / math.sqrt(leaf_side) * random_part).astype(jnp.bfloat16)


def draw_mix_maps(key, part):
    full_shape = (N_GRP, A, N_BLK, N_BLK)
    random_part = jax.random.normal(key, full_shape, jnp.float32)
    identity = jnp.eye(N_BLK, dtype=jnp.float32)
    return (identity + 0.3 / math.sqrt(N_BLK) * random_part).astype(jnp.bfloat16)


def level_of(key, extent, split, low, top_value):
    def one(dim, parts):
        draws = jax.random.uniform(jax.random.fold_in(jax.random.fold_in(key, 6), dim), (parts,), jnp.float32, low / len(split), top_value / len(split))
        return jnp.repeat(jnp.exp(draws), extent[dim] // parts).reshape((-1,) + (1,) * (len(extent) - dim - 1))

    factor_of = one(*split[0])
    for cut in split[1:]:
        factor_of = factor_of * one(*cut)
    return factor_of


def bell_draw(stream_key, extent, deviation, most, shards=(), kind=jnp.bfloat16):
    values = jax.random.normal(stream_key, extent, jnp.float32) * deviation
    if len(shards) > 0:
        values = level_of(stream_key, extent, shards, -0.22, 0.18) * values
    return jnp.clip(values, min=-most, max=most).astype(kind)


def setup_inputs(seed: int = 0) -> dict:
    seeds = jax.random.split(jax.random.key(seed), 4)
    sketch = bell_draw(seeds[0], (R, N), 0.5, 3.0, ((1, 16),))
    leaf_maps = draw_leaf_maps(jax.random.fold_in(seeds[3], 71), 0)
    mix_maps = draw_mix_maps(jax.random.fold_in(seeds[3], 71), 0)
    return dict(sketch=sketch, leaf_maps=leaf_maps, mix_maps=mix_maps)


def apply_section(current, leaf_map, mixing):
    columns, blocks, leaves, sub_rows = current.shape
    low_part = leaves // blocks
    paired = current.reshape(columns, blocks, leaves // 2, 2 * sub_rows).astype(jnp.float32)
    product = jnp.einsum("rdmi,dij->rdmj", paired, leaf_map.astype(jnp.float32)).astype(jnp.bfloat16)
    product = product.reshape(columns, blocks, blocks, low_part, sub_rows).astype(jnp.float32)
    weights = mixing.reshape(blocks, low_part, blocks, blocks).astype(jnp.float32)
    result = jnp.einsum("dlhk,rdklb->rdhlb", weights, product).astype(jnp.bfloat16)
    return jnp.transpose(result, (0, 2, 1, 3, 4)).reshape(columns, blocks, leaves, sub_rows)


def reference(sketch, leaf_maps, mix_maps):
    panel_cols = sketch.reshape(R // 16, 16, N_BLK, A, B)

    def run_chain(current):
        for section_index in range(N_GRP):
            current = apply_section(current, leaf_maps[section_index], mix_maps[section_index])
        return current

    return lax.map(run_chain, panel_cols).reshape(R, N)
```

```python
import functools

import jax
import jax.numpy as jnp
from jax import lax
from jax.experimental import pallas as pl
from jax.experimental.pallas import tpu as pltpu
from jax.sharding import PartitionSpec as P

MESH = pl.DeviceIdType.MESH
TILE = 16
LANES = 128


def chunk_rows(own_cols):
    left, sizes = own_cols, []
    for size in CHUNKS:
        if left >= size:
            sizes.append(size)
            left -= size
    while left > 0:
        sizes.append(min(left, 2 * TILE))
        left -= sizes[-1]
    return sizes


CHUNKS = (16,16,32,64)


def chain_kernel(
    groups, blocks, sizes, sketch_ref, leaf_in, mix_in, out_ref,
    x_vm, send, recv, half, leaf_all, mix_vm, mix_all, weights,
    x_sem, send_sem, recv_sem, own_sem, leaf_send, leaf_recv, mix_send, mix_recv, go_sem,
):
    grp = lax.axis_index("grp")
    blk = lax.axis_index("blk")
    own_cols, row_len = x_vm.shape
    sub = leaf_in.shape[2] // 2
    leaves = row_len // sub
    low = leaves // blocks
    wide = low * sub
    starts = [sum(sizes[:i]) for i in range(len(sizes))]
    big = blocks * TILE

    barrier = pltpu.get_barrier_semaphore()

    def greet(**where):
        pl.semaphore_signal(barrier, inc=1, device_id=where, device_id_type=MESH)

    @pl.when(grp == 0)
    def _():
        for step in range(blocks):
            greet(grp=1, blk=lax.rem(blk + step, blocks))
        for other in range(2, groups):
            greet(grp=other, blk=blk)

    @pl.when(grp > 0)
    def _():
        for step in range(1, groups):
            greet(grp=lax.rem(grp + step, groups), blk=blk)
        for step in range(1, blocks):
            greet(grp=grp, blk=lax.rem(blk + step, blocks))

    own_mix = pltpu.make_async_copy(mix_in.at[0], mix_vm, own_sem.at[0])
    own_leaf = pltpu.make_async_copy(leaf_in.at[0, 0], leaf_all.at[grp], own_sem.at[1])
    own_mix.start()
    own_leaf.start()

    def load(chunk):
        rows = pl.ds(pl.multiple_of(grp * own_cols + starts[chunk], TILE), sizes[chunk])
        return pltpu.make_async_copy(
            sketch_ref.at[rows, :], x_vm.at[pl.ds(starts[chunk], sizes[chunk]), :], x_sem.at[chunk])

    for chunk in range(len(sizes)):
        load(chunk).start()

    own_mix.wait()
    pick = (
        lax.broadcasted_iota(jnp.int32, (blocks, blocks), 0)
        == lax.broadcasted_iota(jnp.int32, (blocks, blocks), 1)
    ).astype(jnp.bfloat16)
    mix_all[grp] = jnp.zeros(mix_all.shape[1:], jnp.bfloat16)
    mix_all[grp, :, pl.ds(0, low * blocks)] = lax.dot_general(
        pick, mix_vm[...].reshape(low * blocks, blocks), (((1,), (1,)), ((), ())),
        preferred_element_type=jnp.float32
    ).astype(jnp.bfloat16)
    def factor_copies(target, owner):
        where = {"grp": target}
        return (
            pltpu.make_async_remote_copy(
                mix_all.at[owner], mix_all.at[owner], mix_send.at[target], mix_recv.at[owner],
                device_id=where, device_id_type=MESH),
            pltpu.make_async_remote_copy(
                leaf_in.at[0, 0], leaf_all.at[owner], leaf_send.at[target], leaf_recv.at[owner],
                device_id=where, device_id_type=MESH),
        )

    def send_factors():
        for step in range(1, groups):
            for copy in factor_copies(lax.rem(grp + step, groups), grp):
                copy.start()

    @pl.when(grp == 0)
    def _():
        pl.semaphore_wait(barrier, groups - 1)
        send_factors()

    @pl.when(grp == 1)
    def _():
        pl.semaphore_wait(barrier, 2 * blocks - 1 + groups - 2)
        pl.semaphore_signal(go_sem, inc=1, device_id={"grp": 0}, device_id_type=MESH)

    @pl.when(grp > 1)
    def _():
        pl.semaphore_wait(barrier, blocks - 1 + groups - 1)

    spread = (
        lax.broadcasted_iota(jnp.int32, (big, blocks), 0) // TILE
        == lax.broadcasted_iota(jnp.int32, (big, blocks), 1)
    ).astype(jnp.bfloat16)
    same = (
        lax.broadcasted_iota(jnp.int32, (big, big), 0) % TILE
        == lax.broadcasted_iota(jnp.int32, (big, big), 1) % TILE
    )
    nums = (((1,), (1,)), ((), ()))
    width = mix_all.shape[2]

    def build_weights(section):
        for l in range(low):
            chosen = (
                lax.broadcasted_iota(jnp.int32, (big, width), 0) // TILE + l * blocks
                == lax.broadcasted_iota(jnp.int32, (big, width), 1)
            ).astype(jnp.bfloat16)
            tall = lax.dot_general(
                chosen, mix_all[section], nums, preferred_element_type=jnp.float32
            ).astype(jnp.bfloat16)
            full = lax.dot_general(tall, spread, nums, preferred_element_type=jnp.float32)
            weights[l] = jnp.where(same, full, 0.0).astype(jnp.bfloat16)

    def compute(section, start, rows):
        unit = pl.ds(start, rows)
        tiles = rows // TILE

        def piece(leaf):
            if section == 0:
                return x_vm[unit, pl.ds(leaf * sub, sub)]
            return recv[section - 1, leaf // low, unit, pl.ds(leaf % low * sub, sub)]

        leaf_map = leaf_all[section]
        per = min(leaves // 2, max(1, 256 // rows))
        for first in range(0, leaves // 2, per):
            lhs = jnp.concatenate(
                [jnp.concatenate([piece(2 * m), piece(2 * m + 1)], axis=1)
                 for m in range(first, first + per)], axis=0)
            product = jnp.dot(
                lhs, leaf_map, preferred_element_type=jnp.float32).astype(jnp.bfloat16)
            for i in range(per):
                for j in range(2):
                    half[2 * (first + i) + j, pl.ds(0, rows), :] = product[
                        i * rows:(i + 1) * rows, j * sub:(j + 1) * sub]

        for l in range(low):
            rhs = jnp.concatenate(
                [jnp.concatenate(
                    [half[k * low + l, pl.ds(t * TILE, TILE), :] for t in range(tiles)], axis=1)
                 for k in range(blocks)], axis=0)
            mixed = jnp.dot(
                weights[l], rhs, preferred_element_type=jnp.float32).astype(jnp.bfloat16)
            for h in range(blocks):
                for t in range(tiles):
                    send[section, h, pl.ds(start + t * TILE, TILE), pl.ds(l * sub, sub)] = mixed[
                        h * TILE:(h + 1) * TILE, t * sub:(t + 1) * sub]

    order = list(range(1, blocks))

    for section in range(groups):
        @pl.when(grp != section)
        def _():
            factor_copies(section, section)[0].wait_recv()

        build_weights(section)

        @pl.when(grp != section)
        def _():
            factor_copies(section, section)[1].wait_recv()

        @pl.when(grp == section)
        def _():
            own_leaf.wait()

        for chunk, (start, rows) in enumerate(zip(starts, sizes)):
            span = pl.ds(start, rows)
            if section == 0:
                load(chunk).wait()
            else:
                arrived = recv.at[section - 1, :, span, :]
                pltpu.make_async_copy(arrived, arrived, recv_sem.at[section - 1, chunk]).wait()

            unit = half.shape[1]
            if rows <= unit:
                compute(section, start, rows)
            else:
                @pl.loop(0, rows // unit)
                def _(i):
                    compute(section, pl.multiple_of(start + i * unit, TILE), unit)

            if section == 0 and chunk == 0:
                @pl.when(grp == 0)
                def _():
                    pl.semaphore_wait(go_sem, 1)

                @pl.when(grp > 0)
                def _():
                    send_factors()

            if section == groups - 1:
                place = out_ref.at[span, pl.ds(pl.multiple_of(blk * wide, sub), wide)]
            else:
                place = recv.at[section, blk, span, :]
            for step in order:
                target = lax.rem(blk + step, blocks)
                pltpu.make_async_remote_copy(
                    send.at[section, target, span, :], place,
                    send_sem.at[section, chunk], recv_sem.at[section, chunk],
                    device_id={"blk": target}, device_id_type=MESH).start()
            pltpu.make_async_copy(
                send.at[section, blk, span, :], place, recv_sem.at[section, chunk]).start()

    for step in range(1, groups):
        for copy in factor_copies(lax.rem(grp + step, groups), grp):
            copy.wait_send()
    for chunk, (start, rows) in enumerate(zip(starts, sizes)):
        span = pl.ds(start, rows)
        for section in range(groups):
            left = send.at[section, pl.ds(0, blocks - 1), span, :]
            pltpu.make_async_copy(left, left, send_sem.at[section, chunk]).wait()
        arrived = out_ref.at[span, :]
        pltpu.make_async_copy(arrived, arrived, recv_sem.at[groups - 1, chunk]).wait()


def on_device(sketch, leaf_maps, mix_maps):
    groups, blocks = lax.axis_size("grp"), lax.axis_size("blk")
    total_cols, rows_dev = sketch.shape
    own_cols = total_cols // groups
    pair = leaf_maps.shape[2]
    sub = pair // 2
    leaves = rows_dev // sub
    low = leaves // blocks
    sizes = chunk_rows(own_cols)
    big = blocks * TILE
    width = -(-low * blocks // LANES) * LANES
    in_hbm = pl.BlockSpec(memory_space=pltpu.HBM)
    dma = pltpu.SemaphoreType.DMA
    bf16 = jnp.bfloat16
    return pl.pallas_call(
        functools.partial(chain_kernel, groups, blocks, sizes),
        out_shape=jax.ShapeDtypeStruct((own_cols, rows_dev), bf16),
        in_specs=[in_hbm, in_hbm, in_hbm],
        out_specs=pl.BlockSpec(memory_space=pl.ANY),
        scratch_shapes=[
            pltpu.VMEM((own_cols, rows_dev), bf16),
            pltpu.VMEM((groups, blocks, own_cols, low * sub), bf16),
            pltpu.VMEM((groups - 1, blocks, own_cols, low * sub), bf16),
            pltpu.VMEM((leaves, 2 * TILE, sub), bf16),
            pltpu.VMEM((groups, pair, pair), bf16),
            pltpu.VMEM((low, blocks, blocks), bf16),
            pltpu.VMEM((groups, blocks, width), bf16),
            pltpu.VMEM((low, big, big), bf16),
            dma((len(sizes),)),
            dma((groups, len(sizes))),
            dma((groups, len(sizes))),
            dma((2,)),
            dma((groups,)), dma((groups,)), dma((groups,)), dma((groups,)),
            pltpu.SemaphoreType.REGULAR,
        ],
        compiler_params=pltpu.CompilerParams(
            collective_id=0, has_side_effects=True, vmem_limit_bytes=48 * 1024 * 1024),
    )(sketch, pltpu.with_memory_space_constraint(leaf_maps, pltpu.HBM), pltpu.with_memory_space_constraint(mix_maps, pltpu.HBM))


def solution(mesh):
    placed = (P(None, "blk"), P("grp", "blk", None, None), P("grp", "blk", None, None))
    return jax.shard_map(
        on_device, mesh=mesh, in_specs=placed, out_specs=P("grp", "blk"), check_vma=False
    )
```

```python
import functools

import jax
import jax.numpy as jnp
from jax import lax
from jax.experimental import pallas as pl
from jax.experimental.pallas import tpu as pltpu
from jax.sharding import PartitionSpec as P

MESH = pl.DeviceIdType.MESH
TILE = 16
LANES = 128
CHUNKS = (16, 16, 32, 64)


def chunk_rows(own_cols):
    left, sizes = own_cols, []
    for size in CHUNKS:
        if left >= size:
            sizes.append(size)
            left -= size
    while left > 0:
        sizes.append(min(left, 2 * TILE))
        left -= sizes[-1]
    return sizes


def chain_kernel(
    groups, blocks, own_cols, sizes, sketch_ref, leaf_in, mix_in, out_ref,
    x_vm, send, recv, half, leaf_all, mix_vm, mix_all, weights, lent,
    x_sem, send_sem, recv_sem, own_sem, leaf_send, leaf_recv, mix_send, mix_recv, lent_sem,
    near_sem, far_sem, all_sem,
):
    grp = lax.axis_index("grp")
    blk = lax.axis_index("blk")
    row_len = x_vm.shape[1]
    sub = leaf_in.shape[2] // 2
    leaves = row_len // sub
    low = leaves // blocks
    wide = low * sub
    starts = [sum(sizes[:i]) for i in range(len(sizes))]
    big = blocks * TILE
    far = blocks * 3 // 4
    width = mix_all.shape[2]
    parts = [pl.ds(i * sub, sub) for i in range(2)]
    split = low % 2 == 0

    lend = split and groups == 2 and len(sizes) > 1
    given = low - 1
    middle = blocks // 2
    lent_to = ((far, blocks), (0, middle))

    def each_half(act):
        for upper in range(2):
            @pl.when((blk >= middle) == bool(upper))
            def _():
                act(*lent_to[upper])

    barrier = pltpu.get_barrier_semaphore()
    for step in range(1, groups):
        pl.semaphore_signal(
            barrier, inc=1, device_id={"grp": lax.rem(grp + step, groups)}, device_id_type=MESH)

    @pl.loop(blk + 1, blocks)
    def _(other):
        pl.semaphore_signal(barrier, inc=1, device_id={"blk": other}, device_id_type=MESH)

    own_mix = pltpu.make_async_copy(mix_in.at[0], mix_vm, own_sem.at[0])
    own_leaf = pltpu.make_async_copy(leaf_in.at[0, 0], leaf_all.at[grp], own_sem.at[1])

    def load(chunk):
        rows = pl.ds(pl.multiple_of(grp * own_cols + starts[chunk], TILE), sizes[chunk])
        return pltpu.make_async_copy(
            sketch_ref.at[rows, :], x_vm.at[pl.ds(starts[chunk], sizes[chunk]), :], x_sem.at[chunk])

    lent_load = pltpu.make_async_copy(
        sketch_ref.at[pl.ds(own_cols + starts[0], sizes[0]), :],
        x_vm.at[pl.ds(own_cols, sizes[0]), :], x_sem.at[len(sizes)])

    own_mix.start()
    own_leaf.start()
    for chunk in range(len(sizes)):
        load(chunk).start()
    if lend:
        @pl.when(grp == 0)
        def _():
            lent_load.start()

    def mix_copy(target, owner):
        return pltpu.make_async_remote_copy(
            mix_all.at[owner], mix_all.at[owner], mix_send.at[target], mix_recv.at[owner],
            device_id={"grp": target}, device_id_type=MESH)

    def leaf_copy(target, owner, part):
        return pltpu.make_async_remote_copy(
            leaf_all.at[owner, :, parts[part]], leaf_all.at[owner, :, parts[part]],
            leaf_send.at[target, part], leaf_recv.at[owner, part],
            device_id={"grp": target}, device_id_type=MESH)

    def send_factors():
        own_leaf.wait()
        for step in range(1, groups):
            target = lax.rem(grp + step, groups)
            mix_copy(target, grp).start()
            for part in range(2):
                leaf_copy(target, grp, part).start()

    spread = (
        lax.broadcasted_iota(jnp.int32, (big, blocks), 0) // TILE
        == lax.broadcasted_iota(jnp.int32, (big, blocks), 1)
    ).astype(jnp.bfloat16)
    same = (
        lax.broadcasted_iota(jnp.int32, (big, big), 0) % TILE
        == lax.broadcasted_iota(jnp.int32, (big, big), 1) % TILE
    )
    nums = (((1,), (1,)), ((), ()))

    def own_mixing():
        own_mix.wait()
        pick = (
            lax.broadcasted_iota(jnp.int32, (blocks, blocks), 0)
            == lax.broadcasted_iota(jnp.int32, (blocks, blocks), 1)
        ).astype(jnp.bfloat16)
        mix_all[grp] = jnp.zeros(mix_all.shape[1:], jnp.bfloat16)
        mix_all[grp, :, pl.ds(0, low * blocks)] = lax.dot_general(
            pick, mix_vm[...].reshape(low * blocks, blocks), nums, preferred_element_type=jnp.float32
        ).astype(jnp.bfloat16)

    def build_weights(section, inner):
        for l in inner:
            chosen = (
                lax.broadcasted_iota(jnp.int32, (big, width), 0) // TILE + l * blocks
                == lax.broadcasted_iota(jnp.int32, (big, width), 1)
            ).astype(jnp.bfloat16)
            tall = lax.dot_general(
                chosen, mix_all[section], nums, preferred_element_type=jnp.float32
            ).astype(jnp.bfloat16)
            full = lax.dot_general(tall, spread, nums, preferred_element_type=jnp.float32)
            weights[l] = jnp.where(same, full, 0.0).astype(jnp.bfloat16)

    def leaf_step(section, start, rows, part=None):
        unit = pl.ds(start, rows)

        def piece(leaf):
            if section == 0:
                return x_vm[unit, pl.ds(leaf * sub, sub)]
            return recv[section - 1, leaf // low, unit, pl.ds(leaf % low * sub, sub)]

        leaf_map = leaf_all[section] if part is None else leaf_all[section, :, parts[part]]
        per = min(leaves // 2, max(1, 256 // rows))
        for first in range(0, leaves // 2, per):
            lhs = jnp.concatenate(
                [jnp.concatenate([piece(2 * m), piece(2 * m + 1)], axis=1)
                 for m in range(first, first + per)], axis=0)
            product = jnp.dot(
                lhs, leaf_map, preferred_element_type=jnp.float32).astype(jnp.bfloat16)
            for i in range(per):
                for j in (range(2) if part is None else (part,)):
                    at = j * sub if part is None else 0
                    half[2 * (first + i) + j, pl.ds(0, rows), :] = product[
                        i * rows:(i + 1) * rows, at:at + sub]

    def mix_step(section, start, rows, inner, goal=None):
        tiles = rows // TILE
        for l in inner:
            rhs = jnp.concatenate(
                [jnp.concatenate(
                    [half[k * low + l, pl.ds(t * TILE, TILE), :] for t in range(tiles)], axis=1)
                 for k in range(blocks)], axis=0)
            mixed = jnp.dot(
                weights[l], rhs, preferred_element_type=jnp.float32).astype(jnp.bfloat16)
            for h in range(blocks):
                for t in range(tiles):
                    tile = mixed[h * TILE:(h + 1) * TILE, t * sub:(t + 1) * sub]
                    if goal is not None:
                        goal[h, pl.ds(t * TILE, TILE), :] = tile
                    else:
                        send[section, h, pl.ds(start + t * TILE, TILE), pl.ds(l * sub, sub)] = tile

    def compute(section, start, rows):
        leaf_step(section, start, rows)
        mix_step(section, start, rows, range(low))

    def place(section, span):
        if section == groups - 1:
            return out_ref.at[span, pl.ds(pl.multiple_of(blk * wide, sub), wide)]
        return recv.at[section, blk, span, :]

    def push(section, chunk, target, inner=None):
        span = pl.ds(starts[chunk], sizes[chunk])
        source, goal = send.at[section, target, span, :], place(section, span)
        if inner is not None:
            source, goal = (ref.at[:, pl.ds(inner * sub, sub)] for ref in (source, goal))
        pltpu.make_async_remote_copy(
            source, goal, send_sem.at[section, chunk], recv_sem.at[section, chunk],
            device_id={"blk": target}, device_id_type=MESH).start()

    def keep(section, chunk):
        span = pl.ds(starts[chunk], sizes[chunk])
        pltpu.make_async_copy(
            send.at[section, blk, span, :], place(section, span), recv_sem.at[section, chunk]).start()

    def push_some(section, chunk, first, last, inner=None):
        @pl.loop(first, last)
        def _(target):
            push(section, chunk, target, inner)

    def push_all(section, chunk, inner=None):
        for step in range(1, blocks):
            push(section, chunk, lax.rem(blk + step, blocks), inner)

    def meet(of_near, of_far):
        if of_near:
            @pl.when(blk < far - 1)
            def _():
                pl.semaphore_wait(near_sem, far - 1 - blk)
        if of_far:
            @pl.when(blk < blocks - 1)
            def _():
                pl.semaphore_wait(far_sem, blocks - lax.max(far, blk + 1))

    def first_chunk():
        start, rows = starts[0], sizes[0]
        load(0).wait()

        @pl.when(grp == 0)
        def _():
            leaf_step(0, start, rows)
            for l in range(low):
                if l > 0:
                    build_weights(0, [l])
                mix_step(0, start, rows, [l])
                push_some(0, 0, 0, blk, l)
            keep(0, 0)
            meet(True, False)
            push_some(0, 0, blk + 1, far)
            meet(False, True)
            push_some(0, 0, lax.max(far, blk + 1), blocks)

        @pl.when(grp > 0)
        def _():

            def share(l):
                mix_step(0, start, rows, [l])
                if lend and l == given:
                    def rest(first, last):
                        push_some(0, 0, 0, lax.min(blk, first), l)
                        push_some(0, 0, blk + 1, first, l)
                        push_some(0, 0, last, blk, l)
                        push_some(0, 0, lax.max(last, blk + 1), blocks, l)
                    each_half(rest)
                else:
                    push_all(0, 0, l)

            meet(True, True)
            if lend:
                pl.semaphore_signal(all_sem, inc=1, device_id={"grp": 0}, device_id_type=MESH)
            for part in range(2):
                leaf_copy(0, 0, part).wait_recv()
                leaf_step(0, start, rows, part)
                if split:
                    for l in range(part, low, 2):
                        share(l)
            if not split:
                for l in range(low):
                    share(l)
            keep(0, 0)

    lent_cols = pl.ds(given * sub, sub)

    def lent_copy(target):
        return pltpu.make_async_remote_copy(
            lent.at[target], recv.at[0, blk, pl.ds(starts[0], sizes[0]), lent_cols],
            lent_sem, recv_sem.at[0, 0],
            device_id={"grp": 1, "blk": target}, device_id_type=MESH)

    def lent_chunk():
        @pl.when(grp == 0)
        def _():
            lent_load.wait()
            leaf_step(0, own_cols, sizes[0], given % 2)
            mix_step(0, own_cols, sizes[0], [given], lent)
            pl.semaphore_wait(all_sem, 1)

            def start(first, last):
                for step in range(last - first):
                    lent_copy(first + lax.rem(blk + step, last - first)).start()
            each_half(start)

    own_mixing()

    @pl.when(grp == 0)
    def _():
        build_weights(0, [0])

    pl.semaphore_wait(barrier, blk + groups - 1)
    send_factors()

    @pl.loop(0, blk)
    def _(other):
        @pl.when(blk < far)
        def _():
            pl.semaphore_signal(near_sem, inc=1, device_id={"blk": other}, device_id_type=MESH)

        @pl.when(blk >= far)
        def _():
            pl.semaphore_signal(far_sem, inc=1, device_id={"blk": other}, device_id_type=MESH)

    @pl.when(grp > 0)
    def _():
        mix_copy(0, 0).wait_recv()
        build_weights(0, range(low))

    for section in range(groups):
        if section > 0:
            @pl.when(grp != section)
            def _():
                mix_copy(section, section).wait_recv()

            build_weights(section, range(low))

        if section > 0:
            @pl.when(grp != section)
            def _():
                for part in range(2):
                    leaf_copy(section, section, part).wait_recv()

        for chunk, (start, rows) in enumerate(zip(starts, sizes)):
            if section == 0 and chunk == 0:
                first_chunk()
                continue
            if section == 0:
                load(chunk).wait()
            else:
                arrived = recv.at[section - 1, :, pl.ds(start, rows), :]
                pltpu.make_async_copy(arrived, arrived, recv_sem.at[section - 1, chunk]).wait()

            unit = half.shape[1]
            if rows <= unit:
                compute(section, start, rows)
            else:
                @pl.loop(0, rows // unit)
                def _(i):
                    compute(section, pl.multiple_of(start + i * unit, TILE), unit)
            push_all(section, chunk)
            keep(section, chunk)
            if section == 0 and chunk == 1 and lend:
                lent_chunk()

    for step in range(1, groups):
        target = lax.rem(grp + step, groups)
        mix_copy(target, grp).wait_send()
        for part in range(2):
            leaf_copy(target, grp, part).wait_send()
    for chunk, (start, rows) in enumerate(zip(starts, sizes)):
        span = pl.ds(start, rows)
        for section in range(groups):
            left = send.at[section, pl.ds(0, blocks - 1), span, :]
            if lend and section == 0 and chunk == 0:
                @pl.when(grp == 0)
                def _():
                    pltpu.make_async_copy(left, left, send_sem.at[section, chunk]).wait()

                    def sent(first, last):
                        part = lent.at[pl.ds(0, last - first)]
                        pltpu.make_async_copy(part, part, lent_sem).wait()
                    each_half(sent)

                @pl.when(grp > 0)
                def _():
                    def sent(first, last):
                        whole = left.at[:, :, pl.ds(0, given * sub)]
                        part = left.at[pl.ds(0, blocks - 1 - (last - first)), :, lent_cols]
                        for piece in (whole, part):
                            pltpu.make_async_copy(piece, piece, send_sem.at[section, chunk]).wait()
                    each_half(sent)
            else:
                pltpu.make_async_copy(left, left, send_sem.at[section, chunk]).wait()
        arrived = out_ref.at[span, :]
        pltpu.make_async_copy(arrived, arrived, recv_sem.at[groups - 1, chunk]).wait()


def on_device(sketch, leaf_maps, mix_maps):
    groups, blocks = lax.axis_size("grp"), lax.axis_size("blk")
    total_cols, rows_dev = sketch.shape
    own_cols = total_cols // groups
    pair = leaf_maps.shape[2]
    sub = pair // 2
    leaves = rows_dev // sub
    low = leaves // blocks
    sizes = chunk_rows(own_cols)
    big = blocks * TILE
    width = -(-low * blocks // LANES) * LANES
    in_hbm = pl.BlockSpec(memory_space=pltpu.HBM)
    dma = pltpu.SemaphoreType.DMA
    bf16 = jnp.bfloat16
    keep = functools.partial(pltpu.with_memory_space_constraint, memory_space=pltpu.HBM)
    return pl.pallas_call(
        functools.partial(chain_kernel, groups, blocks, own_cols, sizes),
        out_shape=jax.ShapeDtypeStruct((own_cols, rows_dev), bf16),
        in_specs=[in_hbm, in_hbm, in_hbm],
        out_specs=pl.BlockSpec(memory_space=pl.ANY),
        scratch_shapes=[
            pltpu.VMEM((own_cols + sizes[0], rows_dev), bf16),
            pltpu.VMEM((groups, blocks, own_cols, low * sub), bf16),
            pltpu.VMEM((groups - 1, blocks, own_cols, low * sub), bf16),
            pltpu.VMEM((leaves, 2 * TILE, sub), bf16),
            pltpu.VMEM((groups, pair, pair), bf16),
            pltpu.VMEM((low, blocks, blocks), bf16),
            pltpu.VMEM((groups, blocks, width), bf16),
            pltpu.VMEM((low, big, big), bf16),
            pltpu.VMEM((blocks, sizes[0], sub), bf16),
            dma((len(sizes) + 1,)),
            dma((groups, len(sizes))),
            dma((groups, len(sizes))),
            dma((2,)),
            dma((groups, 2)), dma((groups, 2)), dma((groups,)), dma((groups,)), dma,
            pltpu.SemaphoreType.REGULAR, pltpu.SemaphoreType.REGULAR, pltpu.SemaphoreType.REGULAR,
        ],
        compiler_params=pltpu.CompilerParams(
            collective_id=0, has_side_effects=True, vmem_limit_bytes=48 * 1024 * 1024),
    )(sketch, keep(leaf_maps), keep(mix_maps))


def solution(mesh):
    placed = (P(None, "blk"), P("grp", "blk", None, None), P("grp", "blk", None, None))
    return jax.shard_map(
        on_device, mesh=mesh, in_specs=placed, out_specs=P("grp", "blk"), check_vma=False
    )
```

```python
import functools

import jax
import jax.numpy as jnp
from jax import lax
from jax.experimental import pallas as pl
from jax.experimental.pallas import tpu as pltpu
from jax.sharding import PartitionSpec as P

MESH = pl.DeviceIdType.MESH
TILE = 16
LANES = 128
CHUNKS = (32, 32, 64)


def chunk_rows(own_cols):
    left, sizes = own_cols, []
    for size in CHUNKS:
        if left >= size:
            sizes.append(size)
            left -= size
    while left > 0:
        sizes.append(min(left, 2 * TILE))
        left -= sizes[-1]
    return sizes


def chain_kernel(
    groups, blocks, own_cols, sizes, sketch_ref, leaf_in, mix_in, out_ref,
    x_vm, send, recv, half, leaf_all, mix_vm, mix_all, weights, lent,
    x_sem, send_sem, recv_sem, own_sem, leaf_send, leaf_recv, mix_send, mix_recv, lent_sem,
    go_sem, all_sem,
):
    grp = lax.axis_index("grp")
    blk = lax.axis_index("blk")
    row_len = x_vm.shape[1]
    sub = leaf_in.shape[2] // 2
    leaves = row_len // sub
    low = leaves // blocks
    wide = low * sub
    starts = [sum(sizes[:i]) for i in range(len(sizes))]
    big = blocks * TILE
    far = blocks * 3 // 4
    width = mix_all.shape[2]
    parts = [pl.ds(i * sub, sub) for i in range(2)]
    split = low % 2 == 0

    lend = split and groups == 2 and len(sizes) > 1
    lent_rows = lent.shape[1]
    given = low - 1
    middle = blocks // 2
    lent_to = ((blocks - middle // 4, blocks), (0, middle // 2))

    def each_half(act):
        for upper in range(2):
            @pl.when((blk >= middle) == bool(upper))
            def _():
                act(*lent_to[upper])

    barrier = pltpu.get_barrier_semaphore()
    for step in range(1, groups):
        pl.semaphore_signal(
            barrier, inc=1, device_id={"grp": lax.rem(grp + step, groups)}, device_id_type=MESH)

    @pl.loop(blk + 1, blocks)
    def _(other):
        pl.semaphore_signal(barrier, inc=1, device_id={"blk": other}, device_id_type=MESH)

    own_mix = pltpu.make_async_copy(mix_in.at[0], mix_vm, own_sem.at[0])
    own_leaf = pltpu.make_async_copy(leaf_in.at[0, 0], leaf_all.at[grp], own_sem.at[1])

    def load(chunk):
        rows = pl.ds(pl.multiple_of(grp * own_cols + starts[chunk], TILE), sizes[chunk])
        return pltpu.make_async_copy(
            sketch_ref.at[rows, :], x_vm.at[pl.ds(starts[chunk], sizes[chunk]), :], x_sem.at[chunk])

    lent_load = pltpu.make_async_copy(
        sketch_ref.at[pl.ds(own_cols, lent_rows), :],
        x_vm.at[pl.ds(own_cols, lent_rows), :], x_sem.at[len(sizes)])

    own_mix.start()
    own_leaf.start()
    for chunk in range(len(sizes)):
        load(chunk).start()
    if lend:
        @pl.when(grp == 0)
        def _():
            lent_load.start()

    def mix_copy(target, owner):
        return pltpu.make_async_remote_copy(
            mix_all.at[owner], mix_all.at[owner], mix_send.at[target], mix_recv.at[owner],
            device_id={"grp": target}, device_id_type=MESH)

    def leaf_copy(target, owner, part):
        return pltpu.make_async_remote_copy(
            leaf_all.at[owner, :, parts[part]], leaf_all.at[owner, :, parts[part]],
            leaf_send.at[target, part], leaf_recv.at[owner, part],
            device_id={"grp": target}, device_id_type=MESH)

    def send_mix():
        for step in range(1, groups):
            mix_copy(lax.rem(grp + step, groups), grp).start()

    def send_leaf(part):
        for step in range(1, groups):
            leaf_copy(lax.rem(grp + step, groups), grp, part).start()

    spread = (
        lax.broadcasted_iota(jnp.int32, (big, blocks), 0) // TILE
        == lax.broadcasted_iota(jnp.int32, (big, blocks), 1)
    ).astype(jnp.bfloat16)
    same = (
        lax.broadcasted_iota(jnp.int32, (big, big), 0) % TILE
        == lax.broadcasted_iota(jnp.int32, (big, big), 1) % TILE
    )
    nums = (((1,), (1,)), ((), ()))

    def own_mixing():
        own_mix.wait()
        pick = (
            lax.broadcasted_iota(jnp.int32, (blocks, blocks), 0)
            == lax.broadcasted_iota(jnp.int32, (blocks, blocks), 1)
        ).astype(jnp.bfloat16)
        mix_all[grp] = jnp.zeros(mix_all.shape[1:], jnp.bfloat16)
        mix_all[grp, :, pl.ds(0, low * blocks)] = lax.dot_general(
            pick, mix_vm[...].reshape(low * blocks, blocks), nums, preferred_element_type=jnp.float32
        ).astype(jnp.bfloat16)

    def build_weights(section, inner):
        for l in inner:
            chosen = (
                lax.broadcasted_iota(jnp.int32, (big, width), 0) // TILE + l * blocks
                == lax.broadcasted_iota(jnp.int32, (big, width), 1)
            ).astype(jnp.bfloat16)
            tall = lax.dot_general(
                chosen, mix_all[section], nums, preferred_element_type=jnp.float32
            ).astype(jnp.bfloat16)
            full = lax.dot_general(tall, spread, nums, preferred_element_type=jnp.float32)
            weights[l] = jnp.where(same, full, 0.0).astype(jnp.bfloat16)

    def leaf_step(section, start, rows, part=None, stage=None):
        unit = pl.ds(start, rows)

        def piece(leaf):
            if section == 0:
                return x_vm[unit, pl.ds(leaf * sub, sub)]
            return recv[section - 1, leaf // low, unit, pl.ds(leaf % low * sub, sub)]

        leaf_map = leaf_all[section] if part is None else leaf_all[section, :, parts[part]]
        pairs = range(leaves // 2) if stage is None else range(stage, leaves // 2, low // 2)
        per = min(len(pairs), max(1, 256 // rows))
        for first in range(0, len(pairs), per):
            lhs = jnp.concatenate(
                [jnp.concatenate([piece(2 * m), piece(2 * m + 1)], axis=1)
                 for m in pairs[first:first + per]], axis=0)
            product = jnp.dot(
                lhs, leaf_map, preferred_element_type=jnp.float32).astype(jnp.bfloat16)
            for i, m in enumerate(pairs[first:first + per]):
                for j in (range(2) if part is None else (part,)):
                    at = j * sub if part is None else 0
                    half[2 * m + j, pl.ds(0, rows), :] = product[
                        i * rows:(i + 1) * rows, at:at + sub]

    def mix_step(section, start, rows, inner, goal=None):
        tiles = rows // TILE
        for l in inner:
            rhs = jnp.concatenate(
                [jnp.concatenate(
                    [half[k * low + l, pl.ds(t * TILE, TILE), :] for t in range(tiles)], axis=1)
                 for k in range(blocks)], axis=0)
            mixed = jnp.dot(
                weights[l], rhs, preferred_element_type=jnp.float32).astype(jnp.bfloat16)
            for h in range(blocks):
                for t in range(tiles):
                    tile = mixed[h * TILE:(h + 1) * TILE, t * sub:(t + 1) * sub]
                    if goal is not None:
                        goal[h, pl.ds(t * TILE, TILE), :] = tile
                    else:
                        send[section, h, pl.ds(start + t * TILE, TILE), pl.ds(l * sub, sub)] = tile

    def compute(section, start, rows):
        leaf_step(section, start, rows)
        mix_step(section, start, rows, range(low))

    def place(section, span):
        if section == groups - 1:
            return out_ref.at[span, pl.ds(pl.multiple_of(blk * wide, sub), wide)]
        return recv.at[section, blk, span, :]

    def push(section, chunk, target, inner=None, rows=None):
        first, count = (0, sizes[chunk]) if rows is None else rows
        span = pl.ds(starts[chunk] + first, count)
        source, goal = send.at[section, target, span, :], place(section, span)
        if inner is not None:
            source, goal = (ref.at[:, pl.ds(inner * sub, sub)] for ref in (source, goal))
        pltpu.make_async_remote_copy(
            source, goal, send_sem.at[section, chunk], recv_sem.at[section, chunk],
            device_id={"blk": target}, device_id_type=MESH).start()

    def keep(section, chunk):
        span = pl.ds(starts[chunk], sizes[chunk])
        pltpu.make_async_copy(
            send.at[section, blk, span, :], place(section, span), recv_sem.at[section, chunk]).start()

    def push_some(section, chunk, first, last, inner=None, rows=None):
        @pl.loop(first, last)
        def _(target):
            push(section, chunk, target, inner, rows)

    def push_all(section, chunk, inner=None):
        base = blk // middle * middle
        side = lax.rem(blk, 4) // 2 * 2
        for step in range(1, middle):
            push(section, chunk, base + lax.rem(blk - base + step, middle), inner)
        for step in range(middle):
            plane, at = step // 4 * 4, step % 4
            push(section, chunk, lax.rem(base + middle, blocks) + plane + lax.rem(side + 2 + at, 4), inner)

    stages = [(i, (2 * i, 2 * i + 1)) for i in range(low // 2)] if split else [(None, range(low))]

    def push_first(inner, rows=None):
        push_some(0, 0, 0, blk, inner, rows)

        @pl.loop(blk + 1, blocks)
        def _(target):
            if inner == 0:
                pl.semaphore_wait(go_sem.at[target], 1)
            push(0, 0, target, inner, rows)

    def tell_lender():
        pl.semaphore_signal(all_sem, inc=1, device_id={"grp": 0}, device_id_type=MESH)

    def enter():
        pl.semaphore_wait(barrier, blk + groups - 1)
        send_mix()

    def announce():
        @pl.loop(0, blk)
        def _(other):
            pl.semaphore_signal(go_sem.at[blk], inc=1, device_id={"blk": other}, device_id_type=MESH)

    def first_chunk():
        start, rows = starts[0], sizes[0]
        own_mixing()

        @pl.when(grp == 0)
        def _():
            own_leaf.wait()
            load(0).wait()
            for stage, inner in stages:
                leaf_step(0, start, rows, None, stage)
                for l in inner:
                    build_weights(0, [l])
                    mix_step(0, start, rows, [l])
                    if l == 0:
                        enter()
                        for part in range(2):
                            send_leaf(part)
                        announce()
                    push_some(0, 0, 0, blk, l)
            keep(0, 0)

            @pl.loop(blk + 1, blocks)
            def _(target):
                pl.semaphore_wait(go_sem.at[target], 1)
                push(0, 0, target)

        @pl.when(grp > 0)
        def _():
            enter()
            announce()
            if lend:
                pl.when(blk >= middle)(tell_lender)
            own_leaf.wait()
            for part in range(2):
                send_leaf(part)
            mix_copy(0, 0).wait_recv()
            build_weights(0, range(low))
            load(0).wait()

            def share(l):
                mix_step(0, start, rows, [l])
                if lend and l == given:
                    def rest(first, last):
                        part = (0, lent_rows)
                        push_some(0, 0, 0, lax.min(blk, first), l, part)
                        push_some(0, 0, blk + 1, first, l, part)
                        push_some(0, 0, last, blk, l, part)
                        push_some(0, 0, lax.max(last, blk + 1), blocks, l, part)
                    if rows > lent_rows:
                        push_first(l, (lent_rows, rows - lent_rows))
                    each_half(rest)
                else:
                    push_first(l)
                if lend and l == 0:
                    pl.when(blk < middle)(tell_lender)

            if split:
                for part in range(2):
                    leaf_copy(0, 0, part).wait_recv()
                    for stage, inner in stages:
                        leaf_step(0, start, rows, part, stage)
                        share(inner[part])
            else:
                for part in range(2):
                    leaf_copy(0, 0, part).wait_recv()
                leaf_step(0, start, rows)
                for l in range(low):
                    share(l)
            keep(0, 0)

    lent_cols = pl.ds(given * sub, sub)

    def lent_copy(target):
        return pltpu.make_async_remote_copy(
            lent.at[target], recv.at[0, blk, pl.ds(0, lent_rows), lent_cols],
            lent_sem, recv_sem.at[0, 0],
            device_id={"grp": 1, "blk": target}, device_id_type=MESH)

    def lent_chunk():
        @pl.when(grp == 0)
        def _():
            lent_load.wait()
            leaf_step(0, own_cols, lent_rows, given % 2)
            mix_step(0, own_cols, lent_rows, [given], lent)
            pl.semaphore_wait(all_sem, 1)

            def start(first, last):
                for step in range(last - first):
                    lent_copy(first + lax.rem(blk + step, last - first)).start()
            each_half(start)

    for section in range(groups):
        if section > 0:
            @pl.when(grp != section)
            def _():
                mix_copy(section, section).wait_recv()

            build_weights(section, range(low))

        if section > 0:
            @pl.when(grp != section)
            def _():
                for part in range(2):
                    leaf_copy(section, section, part).wait_recv()

        for chunk, (start, rows) in enumerate(zip(starts, sizes)):
            if section == 0 and chunk == 0:
                first_chunk()
                continue
            if section == 0:
                load(chunk).wait()
            else:
                arrived = recv.at[section - 1, :, pl.ds(start, rows), :]
                pltpu.make_async_copy(arrived, arrived, recv_sem.at[section - 1, chunk]).wait()

            unit = half.shape[1]
            if rows <= unit:
                compute(section, start, rows)
            else:
                @pl.loop(0, rows // unit)
                def _(i):
                    compute(section, pl.multiple_of(start + i * unit, TILE), unit)
            push_all(section, chunk)
            keep(section, chunk)
            if section == 0 and chunk == 1 and lend:
                lent_chunk()

    for step in range(1, groups):
        target = lax.rem(grp + step, groups)
        mix_copy(target, grp).wait_send()
        for part in range(2):
            leaf_copy(target, grp, part).wait_send()
    for chunk, (start, rows) in enumerate(zip(starts, sizes)):
        span = pl.ds(start, rows)
        for section in range(groups):
            left = send.at[section, pl.ds(0, blocks - 1), span, :]
            if lend and section == 0 and chunk == 0:
                @pl.when(grp == 0)
                def _():
                    pltpu.make_async_copy(left, left, send_sem.at[section, chunk]).wait()

                    def sent(first, last):
                        part = lent.at[pl.ds(0, last - first)]
                        pltpu.make_async_copy(part, part, lent_sem).wait()
                    each_half(sent)

                @pl.when(grp > 0)
                def _():
                    def sent(first, last):
                        whole = left.at[:, :, pl.ds(0, given * sub)]
                        part = left.at[
                            pl.ds(0, blocks - 1 - (last - first)), pl.ds(0, lent_rows), lent_cols]
                        pieces = [whole, part]
                        if rows > lent_rows:
                            pieces.append(left.at[:, pl.ds(lent_rows, rows - lent_rows), lent_cols])
                        for piece in pieces:
                            pltpu.make_async_copy(piece, piece, send_sem.at[section, chunk]).wait()
                    each_half(sent)
            else:
                pltpu.make_async_copy(left, left, send_sem.at[section, chunk]).wait()
        arrived = out_ref.at[span, :]
        pltpu.make_async_copy(arrived, arrived, recv_sem.at[groups - 1, chunk]).wait()


def on_device(sketch, leaf_maps, mix_maps):
    groups, blocks = lax.axis_size("grp"), lax.axis_size("blk")
    total_cols, rows_dev = sketch.shape
    own_cols = total_cols // groups
    pair = leaf_maps.shape[2]
    sub = pair // 2
    leaves = rows_dev // sub
    low = leaves // blocks
    sizes = chunk_rows(own_cols)
    big = blocks * TILE
    width = -(-low * blocks // LANES) * LANES
    in_hbm = pl.BlockSpec(memory_space=pltpu.HBM)
    dma = pltpu.SemaphoreType.DMA
    bf16 = jnp.bfloat16
    keep = functools.partial(pltpu.with_memory_space_constraint, memory_space=pltpu.HBM)
    return pl.pallas_call(
        functools.partial(chain_kernel, groups, blocks, own_cols, sizes),
        out_shape=jax.ShapeDtypeStruct((own_cols, rows_dev), bf16),
        in_specs=[in_hbm, in_hbm, in_hbm],
        out_specs=pl.BlockSpec(memory_space=pl.ANY),
        scratch_shapes=[
            pltpu.VMEM((own_cols + TILE, rows_dev), bf16),
            pltpu.VMEM((groups, blocks, own_cols, low * sub), bf16),
            pltpu.VMEM((groups - 1, blocks, own_cols, low * sub), bf16),
            pltpu.VMEM((leaves, 2 * TILE, sub), bf16),
            pltpu.VMEM((groups, pair, pair), bf16),
            pltpu.VMEM((low, blocks, blocks), bf16),
            pltpu.VMEM((groups, blocks, width), bf16),
            pltpu.VMEM((low, big, big), bf16),
            pltpu.VMEM((blocks, TILE, sub), bf16),
            dma((len(sizes) + 1,)),
            dma((groups, len(sizes))),
            dma((groups, len(sizes))),
            dma((2,)),
            dma((groups, 2)), dma((groups, 2)), dma((groups,)), dma((groups,)), dma,
            pltpu.SemaphoreType.REGULAR((blocks,)), pltpu.SemaphoreType.REGULAR,
        ],
        compiler_params=pltpu.CompilerParams(
            collective_id=0, has_side_effects=True, vmem_limit_bytes=48 * 1024 * 1024),
    )(sketch, keep(leaf_maps), keep(mix_maps))


def solution(mesh):
    placed = (P(None, "blk"), P("grp", "blk", None, None), P("grp", "blk", None, None))
    return jax.shard_map(
        on_device, mesh=mesh, in_specs=placed, out_specs=P("grp", "blk"), check_vma=False
    )
```

```python
import functools

import jax
import jax.numpy as jnp
from jax import lax
from jax.experimental import pallas as pl
from jax.experimental.pallas import tpu as pltpu
from jax.sharding import PartitionSpec as P

MESH = pl.DeviceIdType.MESH
TILE = 16
LANES = 128
CHUNKS = (32, 32, 64)


def chunk_rows(own_cols):
    left, sizes = own_cols, []
    for size in CHUNKS:
        if left >= size:
            sizes.append(size)
            left -= size
    while left > 0:
        sizes.append(min(left, 2 * TILE))
        left -= sizes[-1]
    return sizes


def chain_kernel(
    groups, blocks, own_cols, sizes, sketch_ref, leaf_in, mix_in, out_ref,
    x_vm, send, recv, half, leaf_all, mix_vm, mix_all, weights, lent,
    x_sem, sent_sem, recv_sem, own_sem, leaf_recv, mix_recv,
    go_sem, all_sem,
):
    grp = lax.axis_index("grp")
    blk = lax.axis_index("blk")
    row_len = x_vm.shape[1]
    sub = leaf_in.shape[2] // 2
    leaves = row_len // sub
    low = leaves // blocks
    wide = low * sub
    starts = [sum(sizes[:i]) for i in range(len(sizes))]
    big = blocks * TILE
    far = blocks * 3 // 4
    width = mix_all.shape[2]
    parts = [pl.ds(i * sub, sub) for i in range(2)]
    split = low % 2 == 0

    lend = split and groups == 2 and len(sizes) > 1
    lent_rows = lent.shape[1]
    given = low - 1
    middle = blocks // 2
    pair = 2 - blocks % 2
    lent_to = ((blocks - middle // 4, blocks), (0, middle * 3 // 4))

    def each_half(act):
        for upper in range(2):
            @pl.when((blk >= middle) == bool(upper))
            def _():
                act(*lent_to[upper])

    barrier = pltpu.get_barrier_semaphore()
    for step in range(1, groups):
        pl.semaphore_signal(
            barrier, inc=1, device_id={"grp": lax.rem(grp + step, groups)}, device_id_type=MESH)

    @pl.loop(blk + 1, blocks)
    def _(other):
        pl.semaphore_signal(barrier, inc=1, device_id={"blk": other}, device_id_type=MESH)

    own_mix = pltpu.make_async_copy(mix_in.at[0], mix_vm, own_sem.at[0])
    own_leaf = pltpu.make_async_copy(leaf_in.at[0, 0], leaf_all.at[grp], own_sem.at[1])

    def load(chunk):
        rows = pl.ds(pl.multiple_of(grp * own_cols + starts[chunk], TILE), sizes[chunk])
        return pltpu.make_async_copy(
            sketch_ref.at[rows, :], x_vm.at[pl.ds(starts[chunk], sizes[chunk]), :], x_sem.at[chunk])

    lent_load = pltpu.make_async_copy(
        sketch_ref.at[pl.ds(own_cols, lent_rows), :],
        x_vm.at[pl.ds(own_cols, lent_rows), :], x_sem.at[len(sizes)])

    own_mix.start()
    own_leaf.start()
    for chunk in range(len(sizes)):
        load(chunk).start()
    if lend:
        @pl.when(grp == 0)
        def _():
            lent_load.start()

    def mix_copy(target, owner):
        return pltpu.make_async_remote_copy(
            mix_all.at[owner], mix_all.at[owner], sent_sem, mix_recv.at[owner],
            device_id={"grp": target}, device_id_type=MESH)

    def leaf_copy(target, owner, part):
        return pltpu.make_async_remote_copy(
            leaf_all.at[owner, :, parts[part]], leaf_all.at[owner, :, parts[part]],
            sent_sem, leaf_recv.at[owner, part],
            device_id={"grp": target}, device_id_type=MESH)

    def send_mix():
        for step in range(1, groups):
            mix_copy(lax.rem(grp + step, groups), grp).start()

    def send_leaf(part):
        for step in range(1, groups):
            leaf_copy(lax.rem(grp + step, groups), grp, part).start()

    spread = (
        lax.broadcasted_iota(jnp.int32, (big, blocks), 0) // TILE
        == lax.broadcasted_iota(jnp.int32, (big, blocks), 1)
    ).astype(jnp.bfloat16)
    same = (
        lax.broadcasted_iota(jnp.int32, (big, big), 0) % TILE
        == lax.broadcasted_iota(jnp.int32, (big, big), 1) % TILE
    )
    nums = (((1,), (1,)), ((), ()))

    def own_mixing():
        own_mix.wait()
        pick = (
            lax.broadcasted_iota(jnp.int32, (blocks, blocks), 0)
            == lax.broadcasted_iota(jnp.int32, (blocks, blocks), 1)
        ).astype(jnp.bfloat16)
        mix_all[grp] = jnp.zeros(mix_all.shape[1:], jnp.bfloat16)
        mix_all[grp, :, pl.ds(0, low * blocks)] = lax.dot_general(
            pick, mix_vm[...].reshape(low * blocks, blocks), nums, preferred_element_type=jnp.float32
        ).astype(jnp.bfloat16)

    def build_weights(section, inner):
        for l in inner:
            chosen = (
                lax.broadcasted_iota(jnp.int32, (big, width), 0) // TILE + l * blocks
                == lax.broadcasted_iota(jnp.int32, (big, width), 1)
            ).astype(jnp.bfloat16)
            tall = lax.dot_general(
                chosen, mix_all[section], nums, preferred_element_type=jnp.float32
            ).astype(jnp.bfloat16)
            full = lax.dot_general(tall, spread, nums, preferred_element_type=jnp.float32)
            weights[l] = jnp.where(same, full, 0.0).astype(jnp.bfloat16)

    def leaf_step(section, start, rows, part=None, stage=None):
        unit = pl.ds(start, rows)

        def piece(leaf):
            if section == 0:
                return x_vm[unit, pl.ds(leaf * sub, sub)]
            return recv[section - 1, leaf // low, unit, pl.ds(leaf % low * sub, sub)]

        leaf_map = leaf_all[section] if part is None else leaf_all[section, :, parts[part]]
        pairs = range(leaves // 2) if stage is None else range(stage, leaves // 2, low // 2)
        per = min(len(pairs), max(1, 256 // rows))
        for first in range(0, len(pairs), per):
            lhs = jnp.concatenate(
                [jnp.concatenate([piece(2 * m), piece(2 * m + 1)], axis=1)
                 for m in pairs[first:first + per]], axis=0)
            product = jnp.dot(
                lhs, leaf_map, preferred_element_type=jnp.float32).astype(jnp.bfloat16)
            for i, m in enumerate(pairs[first:first + per]):
                for j in (range(2) if part is None else (part,)):
                    at = j * sub if part is None else 0
                    half[2 * m + j, pl.ds(0, rows), :] = product[
                        i * rows:(i + 1) * rows, at:at + sub]

    def mix_step(section, start, rows, inner, goal=None):
        tiles = rows // TILE
        for l in inner:
            rhs = jnp.concatenate(
                [jnp.concatenate(
                    [half[k * low + l, pl.ds(t * TILE, TILE), :] for t in range(tiles)], axis=1)
                 for k in range(blocks)], axis=0)
            mixed = jnp.dot(
                weights[l], rhs, preferred_element_type=jnp.float32).astype(jnp.bfloat16)
            for h in range(blocks):
                for t in range(tiles):
                    tile = mixed[h * TILE:(h + 1) * TILE, t * sub:(t + 1) * sub]
                    if goal is not None:
                        goal[h, pl.ds(t * TILE, TILE), :] = tile
                    else:
                        send[section, h, pl.ds(start + t * TILE, TILE), pl.ds(l * sub, sub)] = tile

    def compute(section, start, rows):
        leaf_step(section, start, rows)
        mix_step(section, start, rows, range(low))

    def place(section, span):
        if section == groups - 1:
            return out_ref.at[span, pl.ds(pl.multiple_of(blk * wide, sub), wide)]
        return recv.at[section, blk, span, :]

    def push(section, chunk, target, inner=None, rows=None):
        first, count = (0, sizes[chunk]) if rows is None else rows
        span = pl.ds(starts[chunk] + first, count)
        source, goal = send.at[section, target, span, :], place(section, span)
        if inner is not None:
            source, goal = (ref.at[:, pl.ds(inner * sub, sub)] for ref in (source, goal))
        pltpu.make_async_remote_copy(
            source, goal, sent_sem, recv_sem.at[section, chunk],
            device_id={"blk": target}, device_id_type=MESH).start()

    def keep(section, chunk):
        span = pl.ds(starts[chunk], sizes[chunk])
        pltpu.make_async_copy(
            send.at[section, blk, span, :], place(section, span), recv_sem.at[section, chunk]).start()

    def push_some(section, chunk, first, last, inner=None, rows=None):
        @pl.loop(first, last)
        def _(target):
            push(section, chunk, target, inner, rows)

    def push_all(section, chunk, inner=None):
        base = blk // middle * middle
        side = lax.rem(blk, 4) // 2 * 2
        for step in range(1, middle):
            push(section, chunk, base + lax.rem(blk - base + step, middle), inner)
        for step in range(middle):
            plane, at = step // 4 * 4, step % 4
            push(section, chunk, lax.rem(base + middle, blocks) + plane + lax.rem(side + 2 + at, 4), inner)

    stages = [(i, (2 * i, 2 * i + 1)) for i in range(low // 2)] if split else [(None, range(low))]

    def push_upper(inner=None, rows=None, meet=True):
        @pl.when(lax.rem(blk, pair) < pair - 1)
        def _():
            if meet:
                pl.semaphore_wait(go_sem.at[blk // pair], 1)
            push(0, 0, blk + 1, inner, rows)

        @pl.loop(blk // pair + 1, blocks // pair)
        def _(group):
            if meet:
                pl.semaphore_wait(go_sem.at[group], pair)
            for member in range(pair):
                push(0, 0, group * pair + member, inner, rows)

    def push_first(inner, rows=None):
        push_some(0, 0, 0, blk, inner, rows)
        push_upper(inner, rows, inner == 0)

    def tell_lender():
        pl.semaphore_signal(all_sem, inc=1, device_id={"grp": 0}, device_id_type=MESH)

    def enter():
        pl.semaphore_wait(barrier, blk + groups - 1)
        send_mix()

    def announce():
        @pl.loop(0, blk)
        def _(other):
            pl.semaphore_signal(
                go_sem.at[blk // pair], inc=1, device_id={"blk": other}, device_id_type=MESH)

    def first_chunk():
        start, rows = starts[0], sizes[0]
        own_mixing()

        @pl.when(grp == 0)
        def _():
            build_weights(0, [0])
            own_leaf.wait()
            enter()
            for part in range(2):
                send_leaf(part)
            announce()
            load(0).wait()
            for stage, inner in stages:
                leaf_step(0, start, rows, None, stage)
                for l in inner:
                    if l > 0:
                        build_weights(0, [l])
                    mix_step(0, start, rows, [l])
                    push_some(0, 0, 0, blk, l)
            keep(0, 0)

            push_upper()

        @pl.when(grp > 0)
        def _():
            enter()
            announce()
            if lend:
                pl.when(blk >= middle)(tell_lender)
            own_leaf.wait()
            for part in range(2):
                send_leaf(part)
            mix_copy(0, 0).wait_recv()
            build_weights(0, range(low))
            load(0).wait()

            def share(l):
                mix_step(0, start, rows, [l])
                if lend and l == given:
                    def rest(first, last):
                        part = (0, lent_rows)
                        push_some(0, 0, 0, lax.min(blk, first), l, part)
                        push_some(0, 0, blk + 1, first, l, part)
                        push_some(0, 0, last, blk, l, part)
                        push_some(0, 0, lax.max(last, blk + 1), blocks, l, part)
                    if rows > lent_rows:
                        push_first(l, (lent_rows, rows - lent_rows))
                    each_half(rest)
                else:
                    push_first(l)
                if lend and l == 0:
                    pl.when(blk < middle)(tell_lender)

            if split:
                for part in range(2):
                    leaf_copy(0, 0, part).wait_recv()
                    for stage, inner in stages:
                        leaf_step(0, start, rows, part, stage)
                        share(inner[part])
            else:
                for part in range(2):
                    leaf_copy(0, 0, part).wait_recv()
                leaf_step(0, start, rows)
                for l in range(low):
                    share(l)
            keep(0, 0)

    lent_cols = pl.ds(given * sub, sub)

    def lent_copy(target):
        return pltpu.make_async_remote_copy(
            lent.at[target], recv.at[0, blk, pl.ds(0, lent_rows), lent_cols],
            sent_sem, recv_sem.at[0, 0],
            device_id={"grp": 1, "blk": target}, device_id_type=MESH)

    def lent_chunk():
        @pl.when(grp == 0)
        def _():
            lent_load.wait()
            leaf_step(0, own_cols, lent_rows, given % 2)
            mix_step(0, own_cols, lent_rows, [given], lent)
            pl.semaphore_wait(all_sem, 1)

            def start(first, last):
                for step in range(last - first):
                    lent_copy(first + lax.rem(blk + step, last - first)).start()
            each_half(start)

    for section in range(groups):
        if section > 0:
            @pl.when(grp != section)
            def _():
                mix_copy(section, section).wait_recv()

            build_weights(section, range(low))

        if section > 0:
            @pl.when(grp != section)
            def _():
                for part in range(2):
                    leaf_copy(section, section, part).wait_recv()

        for chunk, (start, rows) in enumerate(zip(starts, sizes)):
            if section == 0 and chunk == 0:
                first_chunk()
                continue
            if section == 0:
                load(chunk).wait()
            else:
                arrived = recv.at[section - 1, :, pl.ds(start, rows), :]
                pltpu.make_async_copy(arrived, arrived, recv_sem.at[section - 1, chunk]).wait()

            unit = half.shape[1]
            if rows <= unit:
                compute(section, start, rows)
            else:
                @pl.loop(0, rows // unit)
                def _(i):
                    compute(section, pl.multiple_of(start + i * unit, TILE), unit)
            push_all(section, chunk)
            keep(section, chunk)
            if section == 0 and chunk == 1 and lend:
                lent_chunk()

    def drain(*parts):
        for part in parts:
            pltpu.make_async_copy(part, part, sent_sem).wait()

    for step in range(1, groups):
        drain(mix_all.at[grp], leaf_all.at[grp])
    left = send.at[:, pl.ds(0, blocks - 1)]
    if lend:
        @pl.when(grp == 0)
        def _():
            drain(left)
            each_half(lambda first, last: drain(lent.at[pl.ds(0, last - first)]))

        @pl.when(grp > 0)
        def _():
            top, under = pl.ds(0, lent_rows), pl.ds(lent_rows, own_cols - lent_rows)
            drain(left.at[pl.ds(1, groups - 1)], left.at[0, :, under], left.at[
                0, :, top, pl.ds(0, given * sub)])
            each_half(lambda first, last: drain(
                left.at[0, pl.ds(0, blocks - 1 - (last - first)), top, lent_cols]))
    else:
        drain(left)
    for chunk, (start, rows) in enumerate(zip(starts, sizes)):
        arrived = out_ref.at[pl.ds(start, rows), :]
        pltpu.make_async_copy(arrived, arrived, recv_sem.at[groups - 1, chunk]).wait()


def on_device(sketch, leaf_maps, mix_maps):
    groups, blocks = lax.axis_size("grp"), lax.axis_size("blk")
    total_cols, rows_dev = sketch.shape
    own_cols = total_cols // groups
    pair = leaf_maps.shape[2]
    sub = pair // 2
    leaves = rows_dev // sub
    low = leaves // blocks
    sizes = chunk_rows(own_cols)
    big = blocks * TILE
    width = -(-low * blocks // LANES) * LANES
    in_hbm = pl.BlockSpec(memory_space=pltpu.HBM)
    dma = pltpu.SemaphoreType.DMA
    bf16 = jnp.bfloat16
    keep = functools.partial(pltpu.with_memory_space_constraint, memory_space=pltpu.HBM)
    return pl.pallas_call(
        functools.partial(chain_kernel, groups, blocks, own_cols, sizes),
        out_shape=jax.ShapeDtypeStruct((own_cols, rows_dev), bf16),
        in_specs=[in_hbm, in_hbm, in_hbm],
        out_specs=pl.BlockSpec(memory_space=pl.ANY),
        scratch_shapes=[
            pltpu.VMEM((own_cols + TILE, rows_dev), bf16),
            pltpu.VMEM((groups, blocks, own_cols, low * sub), bf16),
            pltpu.VMEM((groups - 1, blocks, own_cols, low * sub), bf16),
            pltpu.VMEM((leaves, 2 * TILE, sub), bf16),
            pltpu.VMEM((groups, pair, pair), bf16),
            pltpu.VMEM((low, blocks, blocks), bf16),
            pltpu.VMEM((groups, blocks, width), bf16),
            pltpu.VMEM((low, big, big), bf16),
            pltpu.VMEM((blocks, TILE, sub), bf16),
            dma((len(sizes) + 1,)),
            dma,
            dma((groups, len(sizes))),
            dma((2,)), dma((groups, 2)), dma((groups,)),
            pltpu.SemaphoreType.REGULAR((blocks // (2 - blocks % 2),)), pltpu.SemaphoreType.REGULAR,
        ],
        compiler_params=pltpu.CompilerParams(
            collective_id=0, has_side_effects=True, vmem_limit_bytes=48 * 1024 * 1024),
    )(sketch, keep(leaf_maps), keep(mix_maps))


def solution(mesh):
    placed = (P(None, "blk"), P("grp", "blk", None, None), P("grp", "blk", None, None))
    return jax.shard_map(
        on_device, mesh=mesh, in_specs=placed, out_specs=P("grp", "blk"), check_vma=False
    )
```

```python
import functools

import jax
import jax.numpy as jnp
from jax import lax
from jax.experimental import pallas as pl
from jax.experimental.pallas import tpu as pltpu
from jax.sharding import PartitionSpec as P

MESH = pl.DeviceIdType.MESH
TILE = 16
LANES = 128
CHUNKS = (32, 32, 64)


def chunk_rows(own_cols):
    left, sizes = own_cols, []
    for size in CHUNKS:
        if left >= size:
            sizes.append(size)
            left -= size
    while left > 0:
        sizes.append(min(left, 2 * TILE))
        left -= sizes[-1]
    return sizes


def chain_kernel(
    groups, blocks, own_cols, sizes, sketch_ref, leaf_in, mix_in, out_ref,
    x_vm, send, recv, half, leaf_all, mix_vm, mix_all, weights, lent,
    x_sem, sent_sem, recv_sem, own_sem, leaf_recv, mix_recv,
    go_sem, all_sem,
):
    grp = lax.axis_index("grp")
    blk = lax.axis_index("blk")
    row_len = x_vm.shape[1]
    sub = leaf_in.shape[2] // 2
    leaves = row_len // sub
    low = leaves // blocks
    wide = low * sub
    starts = [sum(sizes[:i]) for i in range(len(sizes))]
    big = blocks * TILE
    far = blocks * 3 // 4
    width = mix_all.shape[2]
    parts = [pl.ds(i * sub, sub) for i in range(2)]
    split = low % 2 == 0

    lend = split and groups == 2 and len(sizes) > 1
    lent_rows = lent.shape[1]
    given = low - 1
    middle = blocks // 2
    pair = 2 - blocks % 2
    lent_to = ((blocks - middle // 4, blocks), (0, middle * 3 // 4))

    def each_half(act):
        for upper in range(2):
            @pl.when((blk >= middle) == bool(upper))
            def _():
                act(*lent_to[upper])

    barrier = pltpu.get_barrier_semaphore()
    for step in range(1, groups):
        pl.semaphore_signal(
            barrier, inc=1, device_id={"grp": lax.rem(grp + step, groups)}, device_id_type=MESH)

    @pl.loop(blk + 1, blocks)
    def _(other):
        pl.semaphore_signal(barrier, inc=1, device_id={"blk": other}, device_id_type=MESH)

    own_mix = pltpu.make_async_copy(mix_in.at[0], mix_vm, own_sem.at[0])
    own_leaf = pltpu.make_async_copy(leaf_in.at[0, 0], leaf_all.at[grp], own_sem.at[1])

    def load(chunk):
        rows = pl.ds(pl.multiple_of(grp * own_cols + starts[chunk], TILE), sizes[chunk])
        return pltpu.make_async_copy(
            sketch_ref.at[rows, :], x_vm.at[pl.ds(starts[chunk], sizes[chunk]), :], x_sem.at[chunk])

    lent_load = pltpu.make_async_copy(
        sketch_ref.at[pl.ds(own_cols, lent_rows), :],
        x_vm.at[pl.ds(own_cols, lent_rows), :], x_sem.at[len(sizes)])

    own_mix.start()
    own_leaf.start()
    for chunk in range(len(sizes)):
        load(chunk).start()
    if lend:
        @pl.when(grp == 0)
        def _():
            lent_load.start()

    def mix_copy(target, owner):
        return pltpu.make_async_remote_copy(
            mix_all.at[owner], mix_all.at[owner], sent_sem, mix_recv.at[owner],
            device_id={"grp": target}, device_id_type=MESH)

    def leaf_copy(target, owner, part):
        return pltpu.make_async_remote_copy(
            leaf_all.at[owner, :, parts[part]], leaf_all.at[owner, :, parts[part]],
            sent_sem, leaf_recv.at[owner, part],
            device_id={"grp": target}, device_id_type=MESH)

    def send_mix():
        for step in range(1, groups):
            mix_copy(lax.rem(grp + step, groups), grp).start()

    def send_leaf(part):
        for step in range(1, groups):
            leaf_copy(lax.rem(grp + step, groups), grp, part).start()

    spread = (
        lax.broadcasted_iota(jnp.int32, (big, blocks), 0) // TILE
        == lax.broadcasted_iota(jnp.int32, (big, blocks), 1)
    ).astype(jnp.bfloat16)
    same = (
        lax.broadcasted_iota(jnp.int32, (big, big), 0) % TILE
        == lax.broadcasted_iota(jnp.int32, (big, big), 1) % TILE
    )
    nums = (((1,), (1,)), ((), ()))

    def own_mixing():
        own_mix.wait()
        pick = (
            lax.broadcasted_iota(jnp.int32, (blocks, blocks), 0)
            == lax.broadcasted_iota(jnp.int32, (blocks, blocks), 1)
        ).astype(jnp.bfloat16)
        mix_all[grp] = jnp.zeros(mix_all.shape[1:], jnp.bfloat16)
        mix_all[grp, :, pl.ds(0, low * blocks)] = lax.dot_general(
            pick, mix_vm[...].reshape(low * blocks, blocks), nums, preferred_element_type=jnp.float32
        ).astype(jnp.bfloat16)

    def build_weights(section, inner):
        for l in inner:
            chosen = (
                lax.broadcasted_iota(jnp.int32, (big, width), 0) // TILE + l * blocks
                == lax.broadcasted_iota(jnp.int32, (big, width), 1)
            ).astype(jnp.bfloat16)
            tall = lax.dot_general(
                chosen, mix_all[section], nums, preferred_element_type=jnp.float32
            ).astype(jnp.bfloat16)
            full = lax.dot_general(tall, spread, nums, preferred_element_type=jnp.float32)
            weights[l] = jnp.where(same, full, 0.0).astype(jnp.bfloat16)

    def leaf_step(section, start, rows, part=None, stage=None):
        unit = pl.ds(start, rows)

        def piece(leaf):
            if section == 0:
                return x_vm[unit, pl.ds(leaf * sub, sub)]
            return recv[section - 1, leaf // low, unit, pl.ds(leaf % low * sub, sub)]

        leaf_map = leaf_all[section] if part is None else leaf_all[section, :, parts[part]]
        pairs = range(leaves // 2) if stage is None else range(stage, leaves // 2, low // 2)
        per = min(len(pairs), max(1, 256 // rows))
        for first in range(0, len(pairs), per):
            lhs = jnp.concatenate(
                [jnp.concatenate([piece(2 * m), piece(2 * m + 1)], axis=1)
                 for m in pairs[first:first + per]], axis=0)
            product = jnp.dot(
                lhs, leaf_map, preferred_element_type=jnp.float32).astype(jnp.bfloat16)
            for i, m in enumerate(pairs[first:first + per]):
                for j in (range(2) if part is None else (part,)):
                    at = j * sub if part is None else 0
                    half[2 * m + j, pl.ds(0, rows), :] = product[
                        i * rows:(i + 1) * rows, at:at + sub]

    def mix_step(section, start, rows, inner, goal=None):
        tiles = rows // TILE
        for l in inner:
            rhs = jnp.concatenate(
                [jnp.concatenate(
                    [half[k * low + l, pl.ds(t * TILE, TILE), :] for t in range(tiles)], axis=1)
                 for k in range(blocks)], axis=0)
            mixed = jnp.dot(
                weights[l], rhs, preferred_element_type=jnp.float32).astype(jnp.bfloat16)
            for h in range(blocks):
                for t in range(tiles):
                    tile = mixed[h * TILE:(h + 1) * TILE, t * sub:(t + 1) * sub]
                    if goal is not None:
                        goal[h, pl.ds(t * TILE, TILE), :] = tile
                    else:
                        send[section, h, pl.ds(start + t * TILE, TILE), pl.ds(l * sub, sub)] = tile

    def compute(section, start, rows):
        leaf_step(section, start, rows)
        mix_step(section, start, rows, range(low))

    def place(section, span):
        if section == groups - 1:
            return out_ref.at[span, pl.ds(pl.multiple_of(blk * wide, sub), wide)]
        return recv.at[section, blk, span, :]

    def push(section, chunk, target, inner=None, rows=None):
        first, count = (0, sizes[chunk]) if rows is None else rows
        span = pl.ds(starts[chunk] + first, count)
        source, goal = send.at[section, target, span, :], place(section, span)
        if inner is not None:
            source, goal = (ref.at[:, pl.ds(inner * sub, sub)] for ref in (source, goal))
        pltpu.make_async_remote_copy(
            source, goal, sent_sem, recv_sem.at[section, chunk],
            device_id={"blk": target}, device_id_type=MESH).start()

    def keep(section, chunk):
        span = pl.ds(starts[chunk], sizes[chunk])
        pltpu.make_async_copy(
            send.at[section, blk, span, :], place(section, span), recv_sem.at[section, chunk]).start()

    def push_some(section, chunk, first, last, inner=None, rows=None):
        @pl.loop(first, last)
        def _(target):
            push(section, chunk, target, inner, rows)

    def push_all(section, chunk):
        base = blk // middle * middle
        opposite = lax.rem(base + middle, blocks)
        for step in range(1, middle):
            push(section, chunk, base + lax.rem(blk - base + step, middle))
        if middle % 4:
            for step in range(middle):
                push(section, chunk, opposite + step)
            return
        side = lax.rem(blk, 4) // 2 * 2
        lower = (blk < middle).astype(jnp.int32)
        spots = [(plane, at) for plane in range(middle // 4) for at in range(4)]
        rising = sorted(spots, key=lambda spot: (spot[1], spot[0]))
        falling = sorted(spots, key=lambda spot: (spot[0] * 2 + spot[1], spot[0]))
        for (plane, at), (other_plane, other_at) in zip(rising, falling):
            plane = lower * plane + (1 - lower) * other_plane
            at = lower * (at ^ 1) + (1 - lower) * (other_at ^ 1)
            push(section, chunk, opposite + plane * 4 + lax.rem(side + 2 + at, 4))

    stages = [(i, (2 * i, 2 * i + 1)) for i in range(low // 2)] if split else [(None, range(low))]

    def push_upper(inner=None, rows=None, meet=True):
        @pl.when(lax.rem(blk, pair) < pair - 1)
        def _():
            if meet:
                pl.semaphore_wait(go_sem.at[blk // pair], 1)
            push(0, 0, blk + 1, inner, rows)

        @pl.loop(blk // pair + 1, blocks // pair)
        def _(group):
            if meet:
                pl.semaphore_wait(go_sem.at[group], pair)
            for member in range(pair):
                push(0, 0, group * pair + member, inner, rows)

    def push_first(inner, rows=None):
        push_some(0, 0, 0, blk, inner, rows)
        push_upper(inner, rows, inner == 0)

    def tell_lender():
        pl.semaphore_signal(all_sem, inc=1, device_id={"grp": 0}, device_id_type=MESH)

    def enter():
        pl.semaphore_wait(barrier, blk + groups - 1)
        send_mix()

    def announce():
        @pl.loop(0, blk)
        def _(other):
            pl.semaphore_signal(
                go_sem.at[blk // pair], inc=1, device_id={"blk": other}, device_id_type=MESH)

    def first_chunk():
        start, rows = starts[0], sizes[0]
        own_mixing()

        @pl.when(grp == 0)
        def _():
            build_weights(0, [0])
            own_leaf.wait()
            enter()
            for part in range(2):
                send_leaf(part)
            announce()
            load(0).wait()

            @pl.when(blk >= middle)
            def _():
                for stage, inner in stages:
                    leaf_step(0, start, rows, None, stage)
                    for l in inner:
                        if l > 0:
                            build_weights(0, [l])
                        mix_step(0, start, rows, [l])
                        push_some(0, 0, 0, blk, l)

            @pl.when(blk < middle)
            def _():
                build_weights(0, range(1, low))
                compute(0, start, rows)
                push_some(0, 0, 0, blk)

            keep(0, 0)

            push_upper()

        @pl.when(grp > 0)
        def _():
            enter()
            announce()
            if lend:
                pl.when(blk >= middle)(tell_lender)
            own_leaf.wait()
            for part in range(2):
                send_leaf(part)
            mix_copy(0, 0).wait_recv()
            build_weights(0, range(low))
            load(0).wait()

            def share(l):
                mix_step(0, start, rows, [l])
                if lend and l == given:
                    def rest(first, last):
                        part = (0, lent_rows)
                        push_some(0, 0, 0, lax.min(blk, first), l, part)
                        push_some(0, 0, blk + 1, first, l, part)
                        push_some(0, 0, last, blk, l, part)
                        push_some(0, 0, lax.max(last, blk + 1), blocks, l, part)
                    if rows > lent_rows:
                        push_first(l, (lent_rows, rows - lent_rows))
                    each_half(rest)
                else:
                    push_first(l)
                if lend and l == 0:
                    pl.when(blk < middle)(tell_lender)

            if split:
                for part in range(2):
                    leaf_copy(0, 0, part).wait_recv()
                    for stage, inner in stages:
                        leaf_step(0, start, rows, part, stage)
                        share(inner[part])
            else:
                for part in range(2):
                    leaf_copy(0, 0, part).wait_recv()
                leaf_step(0, start, rows)
                for l in range(low):
                    share(l)
            keep(0, 0)

    lent_cols = pl.ds(given * sub, sub)

    def lent_copy(target):
        return pltpu.make_async_remote_copy(
            lent.at[target], recv.at[0, blk, pl.ds(0, lent_rows), lent_cols],
            sent_sem, recv_sem.at[0, 0],
            device_id={"grp": 1, "blk": target}, device_id_type=MESH)

    def lent_chunk():
        @pl.when(grp == 0)
        def _():
            lent_load.wait()
            leaf_step(0, own_cols, lent_rows, given % 2)
            mix_step(0, own_cols, lent_rows, [given], lent)
            pl.semaphore_wait(all_sem, 1)

            def start(first, last):
                for step in range(last - first):
                    lent_copy(first + lax.rem(blk + step, last - first)).start()
            each_half(start)

    for section in range(groups):
        if section > 0:
            @pl.when(grp != section)
            def _():
                mix_copy(section, section).wait_recv()

            build_weights(section, range(low))

        if section > 0:
            @pl.when(grp != section)
            def _():
                for part in range(2):
                    leaf_copy(section, section, part).wait_recv()

        for chunk, (start, rows) in enumerate(zip(starts, sizes)):
            if section == 0 and chunk == 0:
                first_chunk()
                continue
            if section == 0:
                load(chunk).wait()
            else:
                arrived = recv.at[section - 1, :, pl.ds(start, rows), :]
                pltpu.make_async_copy(arrived, arrived, recv_sem.at[section - 1, chunk]).wait()

            unit = half.shape[1]
            if rows <= unit:
                compute(section, start, rows)
            else:
                @pl.loop(0, rows // unit)
                def _(i):
                    compute(section, pl.multiple_of(start + i * unit, TILE), unit)
            push_all(section, chunk)
            keep(section, chunk)
            if section == 0 and chunk == 1 and lend:
                lent_chunk()

    def drain(*parts):
        for part in parts:
            pltpu.make_async_copy(part, part, sent_sem).wait()

    for step in range(1, groups):
        drain(mix_all.at[grp], leaf_all.at[grp])
    left = send.at[:, pl.ds(0, blocks - 1)]
    if lend:
        @pl.when(grp == 0)
        def _():
            drain(left)
            each_half(lambda first, last: drain(lent.at[pl.ds(0, last - first)]))

        @pl.when(grp > 0)
        def _():
            top, under = pl.ds(0, lent_rows), pl.ds(lent_rows, own_cols - lent_rows)
            drain(left.at[pl.ds(1, groups - 1)], left.at[0, :, under], left.at[
                0, :, top, pl.ds(0, given * sub)])
            each_half(lambda first, last: drain(
                left.at[0, pl.ds(0, blocks - 1 - (last - first)), top, lent_cols]))
    else:
        drain(left)
    for chunk, (start, rows) in enumerate(zip(starts, sizes)):
        arrived = out_ref.at[pl.ds(start, rows), :]
        pltpu.make_async_copy(arrived, arrived, recv_sem.at[groups - 1, chunk]).wait()


def on_device(sketch, leaf_maps, mix_maps):
    groups, blocks = lax.axis_size("grp"), lax.axis_size("blk")
    total_cols, rows_dev = sketch.shape
    own_cols = total_cols // groups
    pair = leaf_maps.shape[2]
    sub = pair // 2
    leaves = rows_dev // sub
    low = leaves // blocks
    sizes = chunk_rows(own_cols)
    big = blocks * TILE
    width = -(-low * blocks // LANES) * LANES
    in_hbm = pl.BlockSpec(memory_space=pltpu.HBM)
    dma = pltpu.SemaphoreType.DMA
    bf16 = jnp.bfloat16
    keep = functools.partial(pltpu.with_memory_space_constraint, memory_space=pltpu.HBM)
    return pl.pallas_call(
        functools.partial(chain_kernel, groups, blocks, own_cols, sizes),
        out_shape=jax.ShapeDtypeStruct((own_cols, rows_dev), bf16),
        in_specs=[in_hbm, in_hbm, in_hbm],
        out_specs=pl.BlockSpec(memory_space=pl.ANY),
        scratch_shapes=[
            pltpu.VMEM((own_cols + TILE, rows_dev), bf16),
            pltpu.VMEM((groups, blocks, own_cols, low * sub), bf16),
            pltpu.VMEM((groups - 1, blocks, own_cols, low * sub), bf16),
            pltpu.VMEM((leaves, 2 * TILE, sub), bf16),
            pltpu.VMEM((groups, pair, pair), bf16),
            pltpu.VMEM((low, blocks, blocks), bf16),
            pltpu.VMEM((groups, blocks, width), bf16),
            pltpu.VMEM((low, big, big), bf16),
            pltpu.VMEM((blocks, TILE, sub), bf16),
            dma((len(sizes) + 1,)),
            dma,
            dma((groups, len(sizes))),
            dma((2,)), dma((groups, 2)), dma((groups,)),
            pltpu.SemaphoreType.REGULAR((blocks // (2 - blocks % 2),)), pltpu.SemaphoreType.REGULAR,
        ],
        compiler_params=pltpu.CompilerParams(
            collective_id=0, has_side_effects=True, vmem_limit_bytes=48 * 1024 * 1024),
    )(sketch, keep(leaf_maps), keep(mix_maps))


def solution(mesh):
    placed = (P(None, "blk"), P("grp", "blk", None, None), P("grp", "blk", None, None))
    return jax.shard_map(
        on_device, mesh=mesh, in_specs=placed, out_specs=P("grp", "blk"), check_vma=False
    )
```

```python
import functools

import jax
import jax.numpy as jnp
from jax import lax
from jax.experimental import pallas as pl
from jax.experimental.pallas import tpu as pltpu
from jax.sharding import PartitionSpec as P

MESH = pl.DeviceIdType.MESH
TILE = 16
LANES = 128
CHUNKS = (32, 32, 64)


def chunk_rows(own_cols):
    left, sizes = own_cols, []
    for size in CHUNKS:
        if left >= size:
            sizes.append(size)
            left -= size
    while left > 0:
        sizes.append(min(left, 2 * TILE))
        left -= sizes[-1]
    return sizes


def chain_kernel(
    groups, blocks, own_cols, sizes, sketch_ref, leaf_in, mix_in, out_ref,
    x_vm, send, recv, half, leaf_all, mix_vm, mix_all, weights, lent,
    x_sem, sent_sem, recv_sem, last_sem, own_sem, leaf_recv, mix_recv,
    go_sem, all_sem,
):
    grp = lax.axis_index("grp")
    blk = lax.axis_index("blk")
    row_len = x_vm.shape[1]
    sub = leaf_in.shape[2] // 2
    leaves = row_len // sub
    low = leaves // blocks
    wide = low * sub
    starts = [sum(sizes[:i]) for i in range(len(sizes))]
    big = blocks * TILE
    far = blocks * 3 // 4
    width = mix_all.shape[2]
    parts = [pl.ds(i * sub, sub) for i in range(2)]
    split = low % 2 == 0

    lend = split and groups == 2 and len(sizes) > 1
    lent_rows = lent.shape[1]
    given = low - 1
    middle = blocks // 2
    pair = 2 - blocks % 2
    lent_to = ((blocks - middle // 4, blocks), (0, middle * 3 // 4))

    def each_half(act):
        for upper in range(2):
            @pl.when((blk >= middle) == bool(upper))
            def _():
                act(*lent_to[upper])

    barrier = pltpu.get_barrier_semaphore()
    for step in range(1, groups):
        pl.semaphore_signal(
            barrier, inc=1, device_id={"grp": lax.rem(grp + step, groups)}, device_id_type=MESH)

    @pl.loop(blk + 1, blocks)
    def _(other):
        pl.semaphore_signal(barrier, inc=1, device_id={"blk": other}, device_id_type=MESH)

    own_mix = pltpu.make_async_copy(mix_in.at[0], mix_vm, own_sem.at[0])
    own_leaf = pltpu.make_async_copy(leaf_in.at[0, 0], leaf_all.at[grp], own_sem.at[1])

    def load(chunk):
        rows = pl.ds(pl.multiple_of(grp * own_cols + starts[chunk], TILE), sizes[chunk])
        return pltpu.make_async_copy(
            sketch_ref.at[rows, :], x_vm.at[pl.ds(starts[chunk], sizes[chunk]), :], x_sem.at[chunk])

    lent_load = pltpu.make_async_copy(
        sketch_ref.at[pl.ds(own_cols, lent_rows), :],
        x_vm.at[pl.ds(own_cols, lent_rows), :], x_sem.at[len(sizes)])

    own_mix.start()
    own_leaf.start()
    for chunk in range(len(sizes)):
        load(chunk).start()
    if lend:
        @pl.when(grp == 0)
        def _():
            lent_load.start()

    def mix_copy(target, owner):
        return pltpu.make_async_remote_copy(
            mix_all.at[owner], mix_all.at[owner], sent_sem, mix_recv.at[owner],
            device_id={"grp": target}, device_id_type=MESH)

    def leaf_copy(target, owner, part):
        return pltpu.make_async_remote_copy(
            leaf_all.at[owner, :, parts[part]], leaf_all.at[owner, :, parts[part]],
            sent_sem, leaf_recv.at[owner, part],
            device_id={"grp": target}, device_id_type=MESH)

    def send_mix():
        for step in range(1, groups):
            mix_copy(lax.rem(grp + step, groups), grp).start()

    def send_leaf(part):
        for step in range(1, groups):
            leaf_copy(lax.rem(grp + step, groups), grp, part).start()

    spread = (
        lax.broadcasted_iota(jnp.int32, (big, blocks), 0) // TILE
        == lax.broadcasted_iota(jnp.int32, (big, blocks), 1)
    ).astype(jnp.bfloat16)
    same = (
        lax.broadcasted_iota(jnp.int32, (big, big), 0) % TILE
        == lax.broadcasted_iota(jnp.int32, (big, big), 1) % TILE
    )
    nums = (((1,), (1,)), ((), ()))

    def own_mixing():
        own_mix.wait()
        pick = (
            lax.broadcasted_iota(jnp.int32, (blocks, blocks), 0)
            == lax.broadcasted_iota(jnp.int32, (blocks, blocks), 1)
        ).astype(jnp.bfloat16)
        mix_all[grp] = jnp.zeros(mix_all.shape[1:], jnp.bfloat16)
        mix_all[grp, :, pl.ds(0, low * blocks)] = lax.dot_general(
            pick, mix_vm[...].reshape(low * blocks, blocks), nums, preferred_element_type=jnp.float32
        ).astype(jnp.bfloat16)

    def build_weights(section, inner):
        for l in inner:
            chosen = (
                lax.broadcasted_iota(jnp.int32, (big, width), 0) // TILE + l * blocks
                == lax.broadcasted_iota(jnp.int32, (big, width), 1)
            ).astype(jnp.bfloat16)
            tall = lax.dot_general(
                chosen, mix_all[section], nums, preferred_element_type=jnp.float32
            ).astype(jnp.bfloat16)
            full = lax.dot_general(tall, spread, nums, preferred_element_type=jnp.float32)
            weights[l] = jnp.where(same, full, 0.0).astype(jnp.bfloat16)

    def leaf_step(section, start, rows, part=None, stage=None):
        unit = pl.ds(start, rows)

        def piece(leaf):
            if section == 0:
                return x_vm[unit, pl.ds(leaf * sub, sub)]
            return recv[section - 1, leaf // low, unit, pl.ds(leaf % low * sub, sub)]

        leaf_map = leaf_all[section] if part is None else leaf_all[section, :, parts[part]]
        pairs = range(leaves // 2) if stage is None else range(stage, leaves // 2, low // 2)
        per = min(len(pairs), max(1, 256 // rows))
        for first in range(0, len(pairs), per):
            lhs = jnp.concatenate(
                [jnp.concatenate([piece(2 * m), piece(2 * m + 1)], axis=1)
                 for m in pairs[first:first + per]], axis=0)
            product = jnp.dot(
                lhs, leaf_map, preferred_element_type=jnp.float32).astype(jnp.bfloat16)
            for i, m in enumerate(pairs[first:first + per]):
                for j in (range(2) if part is None else (part,)):
                    at = j * sub if part is None else 0
                    half[2 * m + j, pl.ds(0, rows), :] = product[
                        i * rows:(i + 1) * rows, at:at + sub]

    def mix_step(section, start, rows, inner, goal=None):
        tiles = rows // TILE
        for l in inner:
            rhs = jnp.concatenate(
                [jnp.concatenate(
                    [half[k * low + l, pl.ds(t * TILE, TILE), :] for t in range(tiles)], axis=1)
                 for k in range(blocks)], axis=0)
            mixed = jnp.dot(
                weights[l], rhs, preferred_element_type=jnp.float32).astype(jnp.bfloat16)
            for h in range(blocks):
                for t in range(tiles):
                    tile = mixed[h * TILE:(h + 1) * TILE, t * sub:(t + 1) * sub]
                    if goal is not None:
                        goal[h, pl.ds(t * TILE, TILE), :] = tile
                    else:
                        send[section, h, pl.ds(start + t * TILE, TILE), pl.ds(l * sub, sub)] = tile

    def compute(section, start, rows):
        leaf_step(section, start, rows)
        mix_step(section, start, rows, range(low))

    def place(section, span):
        if section == groups - 1:
            return out_ref.at[span, pl.ds(pl.multiple_of(blk * wide, sub), wide)]
        return recv.at[section, blk, span, :]

    def landed(section, chunk):
        return last_sem if section == groups - 1 else recv_sem.at[section, chunk]

    def push(section, chunk, target, inner=None, rows=None):
        first, count = (0, sizes[chunk]) if rows is None else rows
        span = pl.ds(starts[chunk] + first, count)
        source, goal = send.at[section, target, span, :], place(section, span)
        if inner is not None:
            source, goal = (ref.at[:, pl.ds(inner * sub, sub)] for ref in (source, goal))
        pltpu.make_async_remote_copy(
            source, goal, sent_sem, landed(section, chunk),
            device_id={"blk": target}, device_id_type=MESH).start()

    def keep(section, chunk):
        span = pl.ds(starts[chunk], sizes[chunk])
        pltpu.make_async_copy(
            send.at[section, blk, span, :], place(section, span), landed(section, chunk)).start()

    def push_some(section, chunk, first, last, inner=None, rows=None):
        @pl.loop(first, last)
        def _(target):
            push(section, chunk, target, inner, rows)

    def push_all(section, chunk):
        base = blk // middle * middle
        opposite = lax.rem(base + middle, blocks)
        for step in range(1, middle):
            push(section, chunk, base + lax.rem(blk - base + step, middle))
        if middle % 4:
            for step in range(middle):
                push(section, chunk, opposite + step)
            return
        side = lax.rem(blk, 4) // 2 * 2
        lower = (blk < middle).astype(jnp.int32)
        spots = [(plane, at) for plane in range(middle // 4) for at in range(4)]
        rising = sorted(spots, key=lambda spot: (spot[1], spot[0]))
        falling = sorted(spots, key=lambda spot: (spot[0] * 2 + spot[1], spot[0]))
        for (plane, at), (other_plane, other_at) in zip(rising, falling):
            plane = lower * plane + (1 - lower) * other_plane
            at = lower * (at ^ 1) + (1 - lower) * (other_at ^ 1)
            push(section, chunk, opposite + plane * 4 + lax.rem(side + 2 + at, 4))

    stages = [(i, (2 * i, 2 * i + 1)) for i in range(low // 2)] if split else [(None, range(low))]

    def push_upper(inner=None, rows=None, meet=True):
        @pl.when(lax.rem(blk, pair) < pair - 1)
        def _():
            if meet:
                pl.semaphore_wait(go_sem.at[blk // pair], 1)
            push(0, 0, blk + 1, inner, rows)

        @pl.loop(blk // pair + 1, blocks // pair)
        def _(group):
            if meet:
                pl.semaphore_wait(go_sem.at[group], pair)
            for member in range(pair):
                push(0, 0, group * pair + member, inner, rows)

    def push_first(inner, rows=None):
        push_some(0, 0, 0, blk, inner, rows)
        push_upper(inner, rows, inner == 0)

    def tell_lender():
        pl.semaphore_signal(all_sem, inc=1, device_id={"grp": 0}, device_id_type=MESH)

    def enter():
        pl.semaphore_wait(barrier, blk + groups - 1)
        send_mix()

    def announce():
        @pl.loop(0, blk)
        def _(other):
            pl.semaphore_signal(
                go_sem.at[blk // pair], inc=1, device_id={"blk": other}, device_id_type=MESH)

    def first_chunk():
        start, rows = starts[0], sizes[0]
        own_mixing()

        @pl.when(grp == 0)
        def _():
            build_weights(0, [0])
            own_leaf.wait()
            enter()
            for part in range(2):
                send_leaf(part)
            announce()
            load(0).wait()

            @pl.when(blk >= middle)
            def _():
                for stage, inner in stages:
                    leaf_step(0, start, rows, None, stage)
                    for l in inner:
                        if l > 0:
                            build_weights(0, [l])
                        mix_step(0, start, rows, [l])
                        push_some(0, 0, 0, blk, l)

            @pl.when(blk < middle)
            def _():
                build_weights(0, range(1, low))
                compute(0, start, rows)
                push_some(0, 0, 0, blk)

            keep(0, 0)

            push_upper()

        @pl.when(grp > 0)
        def _():
            enter()
            announce()
            if lend:
                pl.when(blk >= middle)(tell_lender)
            own_leaf.wait()
            for part in range(2):
                send_leaf(part)
            mix_copy(0, 0).wait_recv()
            build_weights(0, range(low))
            load(0).wait()

            def share(l):
                mix_step(0, start, rows, [l])
                if lend and l == given:
                    def rest(first, last):
                        part = (0, lent_rows)
                        push_some(0, 0, 0, lax.min(blk, first), l, part)
                        push_some(0, 0, blk + 1, first, l, part)
                        push_some(0, 0, last, blk, l, part)
                        push_some(0, 0, lax.max(last, blk + 1), blocks, l, part)
                    if rows > lent_rows:
                        push_first(l, (lent_rows, rows - lent_rows))
                    each_half(rest)
                else:
                    push_first(l)
                if lend and l == 0:
                    pl.when(blk < middle)(tell_lender)

            if split:
                for part in range(2):
                    leaf_copy(0, 0, part).wait_recv()
                    for stage, inner in stages:
                        leaf_step(0, start, rows, part, stage)
                        share(inner[part])
            else:
                for part in range(2):
                    leaf_copy(0, 0, part).wait_recv()
                leaf_step(0, start, rows)
                for l in range(low):
                    share(l)
            keep(0, 0)

    lent_cols = pl.ds(given * sub, sub)

    def lent_copy(target):
        return pltpu.make_async_remote_copy(
            lent.at[target], recv.at[0, blk, pl.ds(0, lent_rows), lent_cols],
            sent_sem, recv_sem.at[0, 0],
            device_id={"grp": 1, "blk": target}, device_id_type=MESH)

    def lent_chunk():
        @pl.when(grp == 0)
        def _():
            lent_load.wait()
            leaf_step(0, own_cols, lent_rows, given % 2)
            mix_step(0, own_cols, lent_rows, [given], lent)
            pl.semaphore_wait(all_sem, 1)

            def start(first, last):
                for step in range(last - first):
                    lent_copy(first + lax.rem(blk + step, last - first)).start()
            each_half(start)

    for section in range(groups):
        if section > 0:
            @pl.when(grp != section)
            def _():
                mix_copy(section, section).wait_recv()

            build_weights(section, range(low))

        if section > 0:
            @pl.when(grp != section)
            def _():
                for part in range(2):
                    leaf_copy(section, section, part).wait_recv()

        for chunk, (start, rows) in enumerate(zip(starts, sizes)):
            if section == 0 and chunk == 0:
                first_chunk()
                continue
            if section == 0:
                load(chunk).wait()
            else:
                arrived = recv.at[section - 1, :, pl.ds(start, rows), :]
                pltpu.make_async_copy(arrived, arrived, recv_sem.at[section - 1, chunk]).wait()

            unit = half.shape[1]
            if rows <= unit:
                compute(section, start, rows)
            else:
                @pl.loop(0, rows // unit)
                def _(i):
                    compute(section, pl.multiple_of(start + i * unit, TILE), unit)
            push_all(section, chunk)
            keep(section, chunk)
            if section == 0 and chunk == 1 and lend:
                lent_chunk()

    def drain(*parts):
        for part in parts:
            pltpu.make_async_copy(part, part, sent_sem).wait()

    for step in range(1, groups):
        drain(mix_all.at[grp], leaf_all.at[grp])
    left = send.at[:, pl.ds(0, blocks - 1)]
    if lend:
        @pl.when(grp == 0)
        def _():
            drain(left)
            each_half(lambda first, last: drain(lent.at[pl.ds(0, last - first)]))

        @pl.when(grp > 0)
        def _():
            top, under = pl.ds(0, lent_rows), pl.ds(lent_rows, own_cols - lent_rows)
            drain(left.at[pl.ds(1, groups - 1)], left.at[0, :, under], left.at[
                0, :, top, pl.ds(0, given * sub)])
            each_half(lambda first, last: drain(
                left.at[0, pl.ds(0, blocks - 1 - (last - first)), top, lent_cols]))
    else:
        drain(left)
    pltpu.make_async_copy(out_ref, out_ref, last_sem).wait()


def on_device(sketch, leaf_maps, mix_maps):
    groups, blocks = lax.axis_size("grp"), lax.axis_size("blk")
    total_cols, rows_dev = sketch.shape
    own_cols = total_cols // groups
    pair = leaf_maps.shape[2]
    sub = pair // 2
    leaves = rows_dev // sub
    low = leaves // blocks
    sizes = chunk_rows(own_cols)
    big = blocks * TILE
    width = -(-low * blocks // LANES) * LANES
    in_hbm = pl.BlockSpec(memory_space=pltpu.HBM)
    dma = pltpu.SemaphoreType.DMA
    bf16 = jnp.bfloat16
    keep = functools.partial(pltpu.with_memory_space_constraint, memory_space=pltpu.HBM)
    return pl.pallas_call(
        functools.partial(chain_kernel, groups, blocks, own_cols, sizes),
        out_shape=jax.ShapeDtypeStruct((own_cols, rows_dev), bf16),
        in_specs=[in_hbm, in_hbm, in_hbm],
        out_specs=pl.BlockSpec(memory_space=pl.ANY),
        scratch_shapes=[
            pltpu.VMEM((own_cols + TILE, rows_dev), bf16),
            pltpu.VMEM((groups, blocks, own_cols, low * sub), bf16),
            pltpu.VMEM((groups - 1, blocks, own_cols, low * sub), bf16),
            pltpu.VMEM((leaves, 2 * TILE, sub), bf16),
            pltpu.VMEM((groups, pair, pair), bf16),
            pltpu.VMEM((low, blocks, blocks), bf16),
            pltpu.VMEM((groups, blocks, width), bf16),
            pltpu.VMEM((low, big, big), bf16),
            pltpu.VMEM((blocks, TILE, sub), bf16),
            dma((len(sizes) + 1,)),
            dma,
            dma((groups - 1, len(sizes))),
            dma,
            dma((2,)), dma((groups, 2)), dma((groups,)),
            pltpu.SemaphoreType.REGULAR((blocks // (2 - blocks % 2),)), pltpu.SemaphoreType.REGULAR,
        ],
        compiler_params=pltpu.CompilerParams(
            collective_id=0, has_side_effects=True, vmem_limit_bytes=48 * 1024 * 1024),
    )(sketch, keep(leaf_maps), keep(mix_maps))


def solution(mesh):
    placed = (P(None, "blk"), P("grp", "blk", None, None), P("grp", "blk", None, None))
    return jax.shard_map(
        on_device, mesh=mesh, in_specs=placed, out_specs=P("grp", "blk"), check_vma=False
    )
```
